32 devices in a mesh: groups: 2 (over y), section: 2 (over core), row: 2 (over x), col: 4 (over z).
Axes of the slice: x: 2, y: 2, z: 4, core: 2. Of those that a mesh axis runs over, the one named last changes fastest.
Arguments:
- mid: bfloat16 [2, 768, 8192], P('section', ('groups', 'col'), 'row'), parts along dimension 1, may hold values from -12000 to 12000
- query_grad: bfloat16 [2, 768, 8192], P('section', ('groups', 'row'), 'col'), parts along dimension 1, may hold values from -6 to 6
- top_grad: bfloat16 [768, 8192], P(('groups', 'col'), 'row'), parts along dimension 0, may hold values from -6 to 6
- w_query: bfloat16 [2, 8192, 8192], P('section', 'row', 'col'), may hold values from -0.0625 to 0.0625
- gain: float32 [2, 8192], P('section', 'row'), may hold values from 0.5 to 1.5
Outputs:
- weight_grad: bfloat16 [4, 8192, 8192], P(('groups', 'section'), 'row', 'col'), parts along dimension 0
- residual_grad: bfloat16 [2, 768, 8192], P('section', ('groups', 'col'), 'row'), parts along dimension 1
The draws below stay inside these ranges and needn't reach their ends.
There are 2 independent parts, one for each index of `groups`. The reference program is written for one: setup_inputs(seed, part) draws one part's arguments, and reference() takes and returns one part's arrays. A program takes and returns all parts, laid end to end along the dimension named above; an argument that names none is the same for every part. Nothing has to cross between parts.
All inputs are finite; a program needn't handle non-finite values.
Results may differ from the reference program's by a relative error of at most 0.0085.
Values may be sent and summed in bfloat16 or wider, within the bound.
A program may use at most 128 MiB of HBM per device.

```python
import math
import jax
import jax.numpy as jnp
from jax import lax

D = 8192
HQ = 8192
TOK = 384
SECTIONS = 2
N_COL = 4


def draw_mid(key, part):
    key_base, key_rows, key_cols, key_tail = jax.random.split(key, 4)
    rise = jnp.exp(math.log(3.0) * jnp.arange(D, dtype=jnp.float32) / (D - 1))
    base = jax.random.truncated_normal(key_base, -4.0, 4.0, (SECTIONS, TOK, D), jnp.float32)
    uniform_tail = jax.random.uniform(key_tail, (SECTIONS, TOK, D), jnp.float32, 0.0001, 1.0)
    heavy = jnp.exp(-0.7 * jnp.log(uniform_tail)) / 10.0
    rows = jnp.exp(jax.random.uniform(key_rows, (SECTIONS, TOK, 1), jnp.float32, math.log(0.5), math.log(5.0)))
    cols = jnp.exp(jax.random.uniform(key_cols, (SECTIONS, 1, D), jnp.float32, math.log(0.4), math.log(4.0)))
    return (base * heavy * rows * cols * rise / math.sqrt(3.0)).astype(jnp.bfloat16)


def with_spikes(drawn, stream_key, source, target, blocks, factor):
    def block_of(axis_at):
        return (jnp.arange(drawn.shape[axis_at]) // (drawn.shape[axis_at] // blocks)).reshape((-1,) + (1,) * (drawn.ndim - 1 - axis_at))

    first = jax.random.permutation(stream_key, blocks)[block_of(target)]
    other_side = (block_of(target) + blocks // 2) % blocks
    return jnp.where((block_of(source) == first) | (block_of(source) == other_side), factor * drawn, drawn)


def shard_levels(rng, extent, pieces, smallest, high):
    level, own = 1.0, jax.random.fold_in(rng, 6)
    for position, blocks in pieces:
        draws = jnp.exp(jax.random.uniform(jax.random.fold_in(own, position), (blocks,), jnp.float32, smallest / len(pieces), high / len(pieces)))
        level = level * jnp.repeat(draws, extent[position] // blocks).reshape([-1 if axis == position else 1 for axis in range(len(extent))])
    return level


def gaussian(stream_key, extent, width, bound, shards=(), held_as=jnp.bfloat16):
    drawn = width * jax.random.normal(stream_key, extent, jnp.float32)
    if shards:
        drawn = drawn * shard_levels(stream_key, extent, shards, -0.22, 0.18)
    return jnp.clip(drawn, -bound, bound).astype(held_as)


def bell_draw_with(own_key, shape, scale, limit, cuts, heavy, kind=jnp.bfloat16):
    drawn = scale * jax.random.normal(own_key, shape, jnp.float32)
    if cuts:
        drawn = drawn * shard_levels(own_key, shape, cuts, -0.22, 0.18)
    return jnp.clip(with_spikes(drawn, jax.random.fold_in(own_key, 3), *heavy), -limit, limit).astype(kind)


def setup_inputs(seed: int = 0, part: int = 0) -> dict:
    key_of = jax.random.split(jax.random.key(seed), 6)
    part_keys = jax.random.split(jax.random.fold_in(key_of[5], part), 6)
    return {
        "mid": draw_mid(jax.random.fold_in(jax.random.fold_in(key_of[5], part), 71), part),
        "query_grad": bell_draw_with(part_keys[1], (SECTIONS, TOK, HQ), 1.0, 6.0, ((0, 2), (1, 2), (2, 4)), (2, 1, 4, 2.0)),
        "top_grad": gaussian(part_keys[2], (TOK, D), 1.0, 6.0, ((0, 4), (1, 2))),
        "w_query": gaussian(key_of[3], (SECTIONS, D, HQ), D ** -0.5, 0.0625, ((0, 2), (1, 2), (2, 4))),
        "gain": jnp.clip(1.0 + 0.1 * jax.random.normal(key_of[4], (SECTIONS, D), jnp.float32), 0.5, 1.5),
    }


EPSILON = 1e-05

def reference(mid, query_grad, top_grad, w_query, gain):
    block = HQ // N_COL
    terms = []
    grads = []
    for layer in range(SECTIONS):
        x_float = mid[layer].astype(jnp.float32)
        gains = gain[layer]
        inverse = lax.rsqrt(lax.optimization_barrier(jnp.sum(x_float * x_float, axis=1)) / D + EPSILON)
        normed = (x_float * inverse[:, None] * gains).astype(jnp.bfloat16)
        normed_grad = jnp.zeros((TOK, D), jnp.float32)
        for index in range(N_COL):
            part_grad = query_grad[layer][:, index * block:(index + 1) * block]
            part_weight = w_query[layer][:, index * block:(index + 1) * block]
            partial_sum = jnp.dot(part_grad, part_weight.T, preferred_element_type=jnp.float32).astype(jnp.bfloat16)
            partial_sum = lax.optimization_barrier(partial_sum)
            normed_grad = normed_grad + partial_sum.astype(jnp.float32)
        product = lax.optimization_barrier(jnp.sum(x_float * gains * normed_grad, axis=1))
        term = inverse[:, None] * gains * normed_grad - x_float * (inverse ** 3 * product / D)[:, None]
        terms.append(term)
        contracted = jnp.dot(normed.T, query_grad[layer], preferred_element_type=jnp.float32)
        grads.append((contracted * TOK ** (-0.5)).astype(jnp.bfloat16))
    total = top_grad.astype(jnp.float32)
    outputs = [None] * SECTIONS
    for layer in range(SECTIONS - 1, -1, -1):
        total = total + terms[layer]
        outputs[layer] = total.astype(jnp.bfloat16)
    return (jnp.stack(grads), jnp.stack(outputs))
```

```python
import functools

import jax
import jax.numpy as jnp
from jax import lax
from jax.experimental import pallas as pl
from jax.experimental.pallas import tpu as pltpu
from jax.sharding import PartitionSpec as P

EPSILON = 1e-05
LANES = 128
ROWS = 16
PIECES = 4
AHEAD = 2
F32 = jnp.float32
BF16 = jnp.bfloat16
MESH = pl.DeviceIdType.MESH


def lane_sums(value):
    total = value[:, :LANES]
    for at in range(LANES, value.shape[1], LANES):
        total = total + value[:, at : at + LANES]
    return total


def diagonal(rows):
    shape = (rows, LANES)
    return lax.broadcasted_iota(jnp.int32, shape, 0) == lax.broadcasted_iota(jnp.int32, shape, 1)


def as_row(column):
    wide = jnp.broadcast_to(column, (column.shape[0], LANES))
    return jnp.sum(jnp.where(diagonal(column.shape[0]), wide, 0.0), axis=0, keepdims=True)


def as_column(row, rows):
    wide = jnp.broadcast_to(row, (rows, LANES))
    return jnp.sum(jnp.where(diagonal(rows), wide, 0.0), axis=1, keepdims=True)


def push(src, dst, send, recv, axis, peer):
    return pltpu.make_async_remote_copy(
        src_ref=src,
        dst_ref=dst,
        send_sem=send,
        recv_sem=recv,
        device_id={axis: peer},
        device_id_type=MESH,
    )


def arrive(ref, sem):
    pltpu.make_async_copy(ref, ref, sem).wait()


def kernel(
    n_sec, n_row, n_col, parts, ahead,
    mid, query, top_hbm, gain_hbm, w_hbm,
    grad_w, res,
    mid_all, query_all, part, from_left, from_right, scaled, gain, gain_column, top,
    squares, squares_in, scales, scale,
    prods, message, message_in, prods_out, prods_in,
    term, later, total,
    mid_sem, query_sem, top_sem, gain_sem, w_sem,
    x_right, x_left, x_recv, right_send, right_recv, left_send, left_recv,
    sq_send, sq_recv, msg_send, msg_recv, pr_send, pr_recv, term_send, term_recv,
):
    me_s, me_r, me_c = (lax.axis_index(a) for a in ("section", "row", "col"))
    tokens, width = mid.shape
    subs, _, depth = query.shape
    fc = width // parts
    tile = min(1024, fc)
    tall = min(256, fc)
    full = width * n_row
    last = n_col - 1
    has_left, has_right = me_c > 0, me_c < last

    def cols(p):
        return pl.ds(p * fc, fc)

    own_query = pl.ds(me_r * subs, subs)
    query_in = pltpu.make_async_copy(query, query_all.at[own_query], query_sem)
    gain_in = pltpu.make_async_copy(gain_hbm, gain, gain_sem)
    top_in = pltpu.make_async_copy(top_hbm, top, top_sem)

    def mid_in(p):
        return pltpu.make_async_copy(mid.at[:, cols(p)], mid_all.at[me_c, p], mid_sem.at[p])

    def w_copy(p):
        rows = pl.ds(pl.multiple_of(p * fc, fc), fc)
        return pltpu.make_async_copy(w_hbm.at[rows], grad_w.at[rows], w_sem.at[p])

    barrier = pltpu.get_barrier_semaphore()

    def greet(axis, peer):
        pl.semaphore_signal(barrier, inc=1, device_id={axis: peer}, device_id_type=MESH)

    for k in range(1, n_row):
        greet("row", lax.rem(me_r + k, n_row))
    pl.when(has_left)(lambda: greet("col", me_c - 1))
    pl.when(has_right)(lambda: greet("col", me_c + 1))
    for k in range(1, n_sec):
        greet("section", lax.rem(me_s + k, n_sec))
    query_in.start()
    gain_in.start()
    for p in range(parts):
        w_copy(p).start()
    for p in range(parts):
        mid_in(p).start()
    top_in.start()
    beside = (me_c + n_col - 1) // n_col + (2 * n_col - 2 - me_c) // n_col
    pl.semaphore_wait(barrier, n_row - 1 + n_sec - 1 + beside)

    def position(right):
        return me_c if right else last - me_c

    def sends(right):
        return has_right if right else has_left

    def receives(right):
        return has_left if right else has_right

    def line(src, dst, right, k, p):
        send, recv = (right_send, right_recv) if right else (left_send, left_recv)
        return push(
            src, dst, send.at[k, p], recv.at[k, p], "col", me_c + 1 if right else me_c - 1
        )

    def mid_copy(right, k, p):
        shard = me_c - k if right else me_c + k
        src = mid.at[:, cols(p)] if k == 0 else mid_all.at[shard, p]
        return line(src, mid_all.at[shard, p], right, k, p)

    def sum_copy(right, k, p):
        shard = me_c + n_col - k if right else me_c - n_col + k
        came = from_left if right else from_right
        return line(part.at[shard, p], came.at[shard, p], right, k, p)

    def start_out(right, k, p):
        if k == 0:
            pl.when(sends(right))(lambda: mid_copy(right, k, p).start())
            return
        early = k <= position(right)
        pl.when(sends(right) & early)(lambda: mid_copy(right, k, p).start())
        pl.when(sends(right) & jnp.logical_not(early))(lambda: sum_copy(right, k, p).start())

    for p in range(parts):
        for right in (True, False):
            start_out(right, 0, p)

    def x_send(k, sub, right):
        piece = me_r - k if right else me_r + k
        shard = piece * subs + sub
        src = query.at[sub] if k == 0 else query_all.at[shard]
        return push(
            src, query_all.at[shard], (x_right if right else x_left).at[shard], x_recv.at[shard],
            "row", me_r + 1 if right else me_r - 1,
        )

    def x_sends(k, right):
        if right:
            return (me_r - k >= 0) & (me_r < n_row - 1)
        return (me_r + k < n_row) & (me_r > 0)

    def sub_of(at, right):
        return at if right else subs - 1 - at

    for right in (True, False):
        pl.when(x_sends(0, right))(lambda: x_send(0, sub_of(0, right), right).start())

    def product(shard, count, load, first):
        def lap(p, _):
            if first:
                w_copy(p).wait()
            for t in range(fc // tile):
                rows = pl.ds(pl.multiple_of(p * fc + t * tile, tile), tile)
                value = lax.dot_general(
                    load(), grad_w[rows, :], (((1,), (1,)), ((), ())), preferred_element_type=F32
                ).astype(BF16)
                for at in range(count):
                    part[shard + at, p, :, t * tile : (t + 1) * tile] = value[
                        at * tokens : (at + 1) * tokens
                    ]
            return 0

        lax.fori_loop(0, parts, lap, 0)

    def over_rows(step, count=tokens // ROWS):
        def lap(i, _):
            step(pl.ds(pl.multiple_of(i * ROWS, ROWS), ROWS))
            return 0

        lax.fori_loop(0, count, lap, 0)

    def sq_copy(k, shard):
        return push(
            squares.at[shard], squares_in.at[me_r, shard], sq_send.at[k, shard],
            sq_recv.at[me_r, shard], "row", lax.rem(me_r + k, n_row),
        )

    def square(shard):
        def step(rows):
            summed = jnp.zeros((ROWS, LANES), F32)
            for p in range(parts):
                value = mid_all[shard, p, rows, :].astype(F32)
                summed = summed + lane_sums(value * value)
            squares[shard, rows, :] = summed

        over_rows(step)
        for k in range(1, n_row):
            sq_copy(k, shard).start()

    def scale_query(shard):
        for k in range(1, n_row):
            peer = lax.rem(me_r + k, n_row)
            arrive(squares_in.at[peer, shard], sq_recv.at[peer, shard])

        def lap(i, _):
            rows = pl.ds(pl.multiple_of(i * ROWS, ROWS), ROWS)
            summed = squares[shard, rows, :]
            for k in range(1, n_row):
                summed = summed + squares_in[lax.rem(me_r + k, n_row), shard, rows, :]
            inverse = lax.rsqrt(jnp.sum(summed, axis=1, keepdims=True) / full + EPSILON)
            scales[shard, rows, :] = jnp.broadcast_to(inverse, (ROWS, LANES))
            at = pl.ds(pl.multiple_of(shard * tokens + i * ROWS, ROWS), ROWS)
            factor = inverse * (n_col * tokens) ** -0.5
            scaled[at, :] = (query_all[shard, rows, :].astype(F32) * factor).astype(BF16)
            return 0

        lax.fori_loop(0, tokens // ROWS, lap, 0)

    def around(k, act):
        pl.when(me_c - k >= 0)(lambda: act(me_c - k))
        pl.when(me_c + k < n_col)(lambda: act(me_c + k))

    def x_step(k, at):
        if k == 1 and at + 1 < subs:
            for right in (True, False):
                @pl.when(x_sends(0, right))
                def _():
                    x_send(0, sub_of(at, right), right).wait_send()
                    x_send(0, sub_of(at + 1, right), right).start()
        for right in (True, False):
            piece = me_r - k if right else me_r + k
            sub = sub_of(at, right)
            shard = piece * subs + sub

            @pl.when((piece >= 0) if right else (piece < n_row))
            def _():
                arrive(query_all.at[shard], x_recv.at[shard])
                if k < n_row - 1:
                    pl.when(x_sends(k, right))(lambda: x_send(k, sub, right).start())
                product(shard, 1, lambda: query_all[shard], False)

    def turn_gain(b, _):
        at = pl.ds(pl.multiple_of(b * LANES, LANES), LANES)
        column = as_column(gain[:, at], LANES)
        gain_column[at, :] = jnp.broadcast_to(column, (LANES, LANES))
        return 0

    def add_products(slot, shard, p):
        def step(rows):
            value = part[shard, p, rows, :].astype(F32) * gain[:, cols(p)]
            prods[slot, rows, :] += lane_sums(mid_all[shard, p, rows, :].astype(F32) * value)

        over_rows(step)

    def take_in(right, k, p):
        came = from_left if right else from_right
        recv = right_recv if right else left_recv
        pl.when(receives(right))(lambda: arrive(came.at[0, p], recv.at[k, p]))

    def add_in(right, k, p):
        if k == last:
            return
        came = from_left if right else from_right
        shard = me_c + last - k if right else me_c - last + k

        @pl.when(receives(right) & (k >= position(right)))
        def _():
            def step(rows):
                part[shard, p, rows, :] = (
                    part[shard, p, rows, :].astype(F32) + came[shard, p, rows, :].astype(F32)
                ).astype(BF16)

            over_rows(step)

    def start_index(right, index):
        if parts <= index < n_col * parts:
            start_out(right, index // parts, index % parts)

    def line_step(k, p):
        index = k * parts + p
        for right in (True, False):
            take_in(right, k, p)
            if ahead < parts:
                start_index(right, index + ahead)
            add_in(right, k, p)
            if ahead >= parts:
                start_index(right, index + ahead)
        if k == n_col - 2:
            pl.when(has_right)(lambda: add_products(1, me_c + 1, p))
            pl.when(has_left)(lambda: add_products(2, me_c - 1, p))

    def message_copy(right):
        slot = 0 if right else 1
        return push(
            message.at[slot], message_in.at[slot], msg_send.at[slot], msg_recv.at[slot],
            "col", me_c + 1 if right else me_c - 1,
        )

    def send_messages():
        for right in (True, False):
            slot = 0 if right else 1

            @pl.when(sends(right))
            def _():
                row = as_row(jnp.sum(prods[slot + 1], axis=1, keepdims=True))
                message[slot] = jnp.broadcast_to(row, (8, LANES))
                message_copy(right).start()

    def pr_copy(k):
        return push(
            prods_out, prods_in.at[me_r], pr_send.at[k], pr_recv.at[me_r],
            "row", lax.rem(me_r + k, n_row),
        )

    def send_products():
        row = as_row(jnp.sum(prods[0], axis=1, keepdims=True))
        prods_out[...] = jnp.broadcast_to(row, (8, LANES))
        for right in (True, False):
            slot = 0 if right else 1

            @pl.when(receives(right))
            def _():
                arrive(message_in.at[slot], msg_recv.at[slot])
                prods_out[...] += message_in[slot]

        for k in range(1, n_row):
            pr_copy(k).start()

    def take_products():
        summed = prods_out[...]
        for k in range(1, n_row):
            peer = lax.rem(me_r + k, n_row)
            arrive(prods_in.at[peer], pr_recv.at[peer])
            summed = summed + prods_in[peer]
        column = as_column(summed[:1], tokens)
        inverse = scales[me_c]
        scale[...] = inverse * inverse * inverse * (column / full)

    def weight(p):
        def lap(t, _):
            at = pl.multiple_of(t * tall, tall)
            left = mid_all[:, p, :, pl.ds(at, tall)].reshape(n_col * tokens, tall)
            value = lax.dot_general(
                left, scaled[...], (((0,), (0,)), ((), ())), preferred_element_type=F32
            )
            rows = pl.ds(pl.multiple_of(p * fc + at, tall), tall)
            factor = gain_column[rows, :]
            for b in range(0, depth, LANES):
                grad_w[rows, b : b + LANES] = (value[:, b : b + LANES] * factor).astype(BF16)
            return 0

        lax.fori_loop(0, fc // tall, lap, 0)

    def term_copy(to, p):
        return push(
            term.at[p], later.at[me_s, p], term_send.at[to, p], term_recv.at[me_s, p],
            "section", to,
        )

    def finish(p):
        def step(rows):
            value = (
                part[me_c, p, rows, :].astype(F32)
                + from_left[me_c, p, rows, :].astype(F32)
                + from_right[me_c, p, rows, :].astype(F32)
            ) * gain[:, cols(p)]
            own = (
                scales[me_c, rows, :][:, :1] * value
                - mid_all[me_c, p, rows, :].astype(F32) * scale[rows, :][:, :1]
            )
            term[p, rows, :] = own.astype(BF16)
            total[p, rows, :] = top[rows, cols(p)].astype(F32) + own

        over_rows(step)
        for to in range(n_sec - 1):
            pl.when(me_s > to)(lambda: term_copy(to, p).start())

    def conclude(p):
        for source in range(1, n_sec):
            @pl.when(me_s < source)
            def _():
                arrive(later.at[source, p], term_recv.at[source, p])

                def step(rows):
                    total[p, rows, :] += later[source, p, rows, :].astype(F32)

                over_rows(step)

        def step(rows):
            res[rows, cols(p)] = total[p, rows, :].astype(BF16)

        over_rows(step)

    query_in.wait()
    product(
        me_r * subs, subs, lambda: query_all[own_query].reshape(subs * tokens, depth), True
    )
    for p in range(parts):
        mid_in(p).wait()
    square(me_c)
    gain_in.wait()
    prods[...] = jnp.zeros(prods.shape, F32)

    @pl.when(jnp.logical_not(has_left))
    def _():
        from_left[me_c] = jnp.zeros(from_left.shape[1:], BF16)

    @pl.when(jnp.logical_not(has_right))
    def _():
        from_right[me_c] = jnp.zeros(from_right.shape[1:], BF16)

    steps = [(k, at) for k in range(1, n_row) for at in range(subs)]
    held = steps[-1:] if subs > 1 and n_col > 1 else []
    for k, at in steps[: len(steps) - len(held)]:
        x_step(k, at)
    if n_col > 1:
        for p in range(parts):
            line_step(0, p)
    for k, at in held:
        x_step(k, at)
    if n_col > 2:
        around(1, square)
    lax.fori_loop(0, width // LANES, turn_gain, 0)
    for p in range(parts):
        add_products(0, me_c, p)
    scale_query(me_c)
    for k in range(1, last):
        for p in range(parts):
            line_step(k, p)
        if k + 1 < last:
            around(k + 1, square)
        if k + 1 == last:
            send_messages()
            around(last, square)
        around(k, scale_query)
    if n_col == 2:
        send_messages()
        around(1, square)
    if n_col > 1:
        around(last, scale_query)
    top_in.wait()
    done = 0
    for p in range(parts):
        weight(p)
        if n_col > 1:
            line_step(last, p)
        if p == parts // 4:
            send_products()
        if p == parts // 2:
            take_products()
        if p >= parts // 2:
            while done <= p:
                finish(done)
                done += 1
    for p in range(parts):
        conclude(p)

    for right in (True, False):
        for k in range(n_row - 1):
            @pl.when(x_sends(k, right))
            def _():
                for at in range(subs - 1 if k == 0 else 0, subs):
                    x_send(k, sub_of(at, right), right).wait_send()

        @pl.when(sends(right))
        def _():
            send = right_send if right else left_send
            for k in range(n_col):
                for p in range(parts):
                    arrive(part.at[0, p], send.at[k, p])
            message_copy(right).wait_send()
    for k in range(1, n_row):
        for shard in range(n_col):
            sq_copy(k, shard).wait_send()
        pr_copy(k).wait_send()
    for to in range(n_sec - 1):
        @pl.when(me_s > to)
        def _():
            for p in range(parts):
                term_copy(to, p).wait_send()


def write_out(pieces, grad_w, res, grad_out, res_out, sem):
    tall = grad_w.shape[0] // pieces
    copies = [
        pltpu.make_async_copy(
            grad_w.at[pl.ds(i * tall, tall)], grad_out.at[pl.ds(i * tall, tall)], sem.at[i]
        )
        for i in range(pieces)
    ]
    copies.append(pltpu.make_async_copy(res, res_out, sem.at[pieces]))
    for copy in copies:
        copy.start()
    for copy in copies:
        copy.wait()


def body(mid, query_grad, top_grad, w_query, gain):
    n_sec, n_row, n_col = (lax.axis_size(a) for a in ("section", "row", "col"))
    tokens, width = mid.shape[1:]
    rows, depth = query_grad.shape[1:]
    subs = rows // tokens
    parts = PIECES
    fc = width // parts
    hbm = pl.BlockSpec(memory_space=pltpu.HBM)
    anywhere = pl.BlockSpec(memory_space=pl.ANY)
    in_vmem = pl.BlockSpec(memory_space=pltpu.VMEM)
    dma = pltpu.SemaphoreType.DMA
    vmem = pltpu.VMEM
    grad_w, res = pl.pallas_call(
        functools.partial(kernel, n_sec, n_row, n_col, parts, AHEAD),
        out_shape=(vmem((width, depth), BF16), vmem((tokens, width), BF16)),
        in_specs=[hbm] * 5,
        out_specs=(in_vmem, in_vmem),
        scratch_shapes=[
            vmem((n_col, parts, tokens, fc), BF16),
            vmem((n_col, tokens, depth), BF16),
            vmem((n_col, parts, tokens, fc), BF16),
            vmem((n_col, parts, tokens, fc), BF16),
            vmem((n_col, parts, tokens, fc), BF16),
            vmem((n_col * tokens, depth), BF16),
            vmem((1, width), F32),
            vmem((width, LANES), F32),
            vmem((tokens, width), BF16),
            vmem((n_col, tokens, LANES), F32),
            vmem((n_row, n_col, tokens, LANES), F32),
            vmem((n_col, tokens, LANES), F32),
            vmem((tokens, LANES), F32),
            vmem((3, tokens, LANES), F32),
            vmem((2, 8, LANES), F32),
            vmem((2, 8, LANES), F32),
            vmem((8, LANES), F32),
            vmem((n_row, 8, LANES), F32),
            vmem((parts, tokens, fc), BF16),
            vmem((n_sec, parts, tokens, fc), BF16),
            vmem((parts, tokens, fc), F32),
            dma((parts,)), dma, dma, dma, dma((parts,)),
            dma((n_col,)), dma((n_col,)), dma((n_col,)),
            dma((n_col, parts)), dma((n_col, parts)),
            dma((n_col, parts)), dma((n_col, parts)),
            dma((n_row, n_col)), dma((n_row, n_col)),
            dma((2,)), dma((2,)), dma((n_row,)), dma((n_row,)),
            dma((n_sec, parts)), dma((n_sec, parts)),
        ],
        compiler_params=pltpu.CompilerParams(
            collective_id=0, has_side_effects=True, vmem_limit_bytes=40 * 1024 * 1024
        ),
    )(mid[0], query_grad[0].reshape(subs, tokens, depth), top_grad, gain, w_query[0])
    pieces = 8
    weight_grad, residual = pl.pallas_call(
        functools.partial(write_out, pieces),
        out_shape=(
            jax.ShapeDtypeStruct((width, depth), BF16),
            jax.ShapeDtypeStruct((tokens, width), BF16),
        ),
        in_specs=[anywhere] * 2,
        out_specs=(anywhere, anywhere),
        scratch_shapes=[dma((pieces + 1,))],
        compiler_params=pltpu.CompilerParams(vmem_limit_bytes=2 * 1024 * 1024),
    )(grad_w, res)
    return (weight_grad[None], residual[None])


def solution(mesh):
    return jax.shard_map(
        body,
        mesh=mesh,
        in_specs=(
            P("section", ("groups", "col"), "row"),
            P("section", ("groups", "row"), "col"),
            P(("groups", "col"), "row"),
            P("section", "row", "col"),
            P("section", "row"),
        ),
        out_specs=(P(("groups", "section"), "row", "col"), P("section", ("groups", "col"), "row")),
        check_vma=False,
    )
```

```python
import functools

import jax
import jax.numpy as jnp
from jax import lax
from jax.experimental import pallas as pl
from jax.experimental.pallas import tpu as pltpu
from jax.sharding import PartitionSpec as P

EPSILON = 1e-05
LANES = 128
ROWS = 16
PIECES = 4
AHEAD = 2
F32 = jnp.float32
BF16 = jnp.bfloat16
MESH = pl.DeviceIdType.MESH


def lane_sums(value):
    total = value[:, :LANES]
    for at in range(LANES, value.shape[1], LANES):
        total = total + value[:, at : at + LANES]
    return total


def diagonal(rows):
    shape = (rows, LANES)
    return lax.broadcasted_iota(jnp.int32, shape, 0) == lax.broadcasted_iota(jnp.int32, shape, 1)


def as_row(column):
    wide = jnp.broadcast_to(column, (column.shape[0], LANES))
    return jnp.sum(jnp.where(diagonal(column.shape[0]), wide, 0.0), axis=0, keepdims=True)


def as_column(row, rows):
    wide = jnp.broadcast_to(row, (rows, LANES))
    return jnp.sum(jnp.where(diagonal(rows), wide, 0.0), axis=1, keepdims=True)


def push(src, dst, send, recv, axis, peer):
    return pltpu.make_async_remote_copy(
        src_ref=src,
        dst_ref=dst,
        send_sem=send,
        recv_sem=recv,
        device_id={axis: peer},
        device_id_type=MESH,
    )


def arrive(ref, sem):
    pltpu.make_async_copy(ref, ref, sem).wait()


def kernel(
    n_sec, n_row, n_col, parts, ahead,
    mid, query, top_hbm, gain_hbm, w_hbm,
    grad_w, res,
    mid_all, query_all, part, from_left, from_right, scaled, gain, gain_column, top,
    squares, squares_in, scales, scale,
    prods, message, message_in, prods_out, prods_in,
    term, later, total,
    mid_sem, query_sem, top_sem, gain_sem, w_sem,
    x_right, x_left, x_recv, right_send, right_recv, left_send, left_recv,
    sq_send, sq_recv, msg_send, msg_recv, pr_send, pr_recv, term_send, term_recv,
):
    me_s, me_r, me_c = (lax.axis_index(a) for a in ("section", "row", "col"))
    tokens, width = mid.shape
    subs, _, depth = query.shape
    fc = width // parts
    tile = min(1024, fc)
    block = min(512, depth)
    full = width * n_row
    last = n_col - 1
    has_left, has_right = me_c > 0, me_c < last

    def cols(p):
        return pl.ds(p * fc, fc)

    own_query = pl.ds(me_r * subs, subs)
    query_in = pltpu.make_async_copy(query, query_all.at[own_query], query_sem)
    gain_in = pltpu.make_async_copy(gain_hbm, gain, gain_sem)
    top_in = pltpu.make_async_copy(top_hbm, top, top_sem)

    def mid_in(p):
        return pltpu.make_async_copy(mid.at[:, cols(p)], mid_all.at[me_c, p], mid_sem.at[p])

    def w_copy(p):
        rows = pl.ds(pl.multiple_of(p * fc, fc), fc)
        return pltpu.make_async_copy(w_hbm.at[rows], grad_w.at[rows], w_sem.at[p])

    barrier = pltpu.get_barrier_semaphore()

    def greet(axis, peer):
        pl.semaphore_signal(barrier, inc=1, device_id={axis: peer}, device_id_type=MESH)

    for k in range(1, n_row):
        greet("row", lax.rem(me_r + k, n_row))
    pl.when(has_left)(lambda: greet("col", me_c - 1))
    pl.when(has_right)(lambda: greet("col", me_c + 1))
    for k in range(1, n_sec):
        greet("section", lax.rem(me_s + k, n_sec))
    query_in.start()
    gain_in.start()
    for p in range(parts):
        w_copy(p).start()
    for p in range(parts):
        mid_in(p).start()
    top_in.start()
    beside = (me_c + n_col - 1) // n_col + (2 * n_col - 2 - me_c) // n_col
    pl.semaphore_wait(barrier, n_row - 1 + n_sec - 1 + beside)

    def position(right):
        return me_c if right else last - me_c

    def sends(right):
        return has_right if right else has_left

    def receives(right):
        return has_left if right else has_right

    def line(src, dst, right, k, p):
        send, recv = (right_send, right_recv) if right else (left_send, left_recv)
        return push(
            src, dst, send.at[k, p], recv.at[k, p], "col", me_c + 1 if right else me_c - 1
        )

    def mid_copy(right, k, p):
        shard = me_c - k if right else me_c + k
        src = mid.at[:, cols(p)] if k == 0 else mid_all.at[shard, p]
        return line(src, mid_all.at[shard, p], right, k, p)

    def sum_copy(right, k, p):
        shard = me_c + n_col - k if right else me_c - n_col + k
        came = from_left if right else from_right
        return line(part.at[shard, p], came.at[shard, p], right, k, p)

    def start_out(right, k, p):
        if k == 0:
            pl.when(sends(right))(lambda: mid_copy(right, k, p).start())
            return
        early = k <= position(right)
        pl.when(sends(right) & early)(lambda: mid_copy(right, k, p).start())
        pl.when(sends(right) & jnp.logical_not(early))(lambda: sum_copy(right, k, p).start())

    for p in range(parts):
        for right in (True, False):
            start_out(right, 0, p)

    def x_send(k, sub, right):
        piece = me_r - k if right else me_r + k
        shard = piece * subs + sub
        src = query.at[sub] if k == 0 else query_all.at[shard]
        return push(
            src, query_all.at[shard], (x_right if right else x_left).at[shard], x_recv.at[shard],
            "row", me_r + 1 if right else me_r - 1,
        )

    def x_sends(k, right):
        if right:
            return (me_r - k >= 0) & (me_r < n_row - 1)
        return (me_r + k < n_row) & (me_r > 0)

    def sub_of(at, right):
        return at if right else subs - 1 - at

    for right in (True, False):
        pl.when(x_sends(0, right))(lambda: x_send(0, sub_of(0, right), right).start())

    def product(shard, count, load, p):
        for t in range(fc // tile):
            rows = pl.ds(pl.multiple_of(p * fc + t * tile, tile), tile)
            value = lax.dot_general(
                load(), grad_w[rows, :], (((1,), (1,)), ((), ())), preferred_element_type=F32
            ).astype(BF16)
            for at in range(count):
                part[shard + at, p, :, t * tile : (t + 1) * tile] = value[
                    at * tokens : (at + 1) * tokens
                ]

    def over_rows(step, count=tokens // ROWS):
        def lap(i, _):
            step(pl.ds(pl.multiple_of(i * ROWS, ROWS), ROWS))
            return 0

        lax.fori_loop(0, count, lap, 0)

    def sq_copy(k, shard):
        return push(
            squares.at[shard], squares_in.at[me_r, shard], sq_send.at[k, shard],
            sq_recv.at[me_r, shard], "row", lax.rem(me_r + k, n_row),
        )

    def square(shard):
        def step(rows):
            summed = jnp.zeros((ROWS, LANES), F32)
            for p in range(parts):
                value = mid_all[shard, p, rows, :].astype(F32)
                summed = summed + lane_sums(value * value)
            squares[shard, rows, :] = summed

        over_rows(step)
        for k in range(1, n_row):
            sq_copy(k, shard).start()

    def scale_query(shard):
        for k in range(1, n_row):
            peer = lax.rem(me_r + k, n_row)
            arrive(squares_in.at[peer, shard], sq_recv.at[peer, shard])

        def lap(i, _):
            rows = pl.ds(pl.multiple_of(i * ROWS, ROWS), ROWS)
            summed = squares[shard, rows, :]
            for k in range(1, n_row):
                summed = summed + squares_in[lax.rem(me_r + k, n_row), shard, rows, :]
            inverse = lax.rsqrt(jnp.sum(summed, axis=1, keepdims=True) / full + EPSILON)
            scales[shard, rows, :] = jnp.broadcast_to(inverse, (ROWS, LANES))
            at = pl.ds(pl.multiple_of(shard * tokens + i * ROWS, ROWS), ROWS)
            factor = inverse * (n_col * tokens) ** -0.5
            scaled[at, :] = (query_all[shard, rows, :].astype(F32) * factor).astype(BF16)
            return 0

        lax.fori_loop(0, tokens // ROWS, lap, 0)

    def around(k, act):
        pl.when(me_c - k >= 0)(lambda: act(me_c - k))
        pl.when(me_c + k < n_col)(lambda: act(me_c + k))

    def x_next(at):
        for right in (True, False):
            @pl.when(x_sends(0, right))
            def _():
                x_send(0, sub_of(at, right), right).wait_send()
                x_send(0, sub_of(at + 1, right), right).start()

    def x_shards(k, at):
        for right in (True, False):
            piece = me_r - k if right else me_r + k
            sub = sub_of(at, right)
            yield right, piece * subs + sub, sub, (piece >= 0) if right else (piece < n_row)

    def x_arrive(k, at):
        for right, shard, sub, valid in x_shards(k, at):
            @pl.when(valid)
            def _():
                arrive(query_all.at[shard], x_recv.at[shard])
                if k < n_row - 1:
                    pl.when(x_sends(k, right))(lambda: x_send(k, sub, right).start())

    def x_product(k, at, p):
        for _, shard, _, valid in x_shards(k, at):
            pl.when(valid)(lambda: product(shard, 1, lambda: query_all[shard], p))

    def turn_gain(b, _):
        at = pl.ds(pl.multiple_of(b * LANES, LANES), LANES)
        column = as_column(gain[:, at], LANES)
        gain_column[at, :] = jnp.broadcast_to(column, (LANES, LANES))
        return 0

    def add_products(slot, shard, p):
        def step(rows):
            value = part[shard, p, rows, :].astype(F32) * gain[:, cols(p)]
            prods[slot, rows, :] += lane_sums(mid_all[shard, p, rows, :].astype(F32) * value)

        over_rows(step)

    def take_in(right, k, p):
        came = from_left if right else from_right
        recv = right_recv if right else left_recv
        pl.when(receives(right))(lambda: arrive(came.at[0, p], recv.at[k, p]))

    def add_in(right, k, p):
        if k == last:
            return
        came = from_left if right else from_right
        shard = me_c + last - k if right else me_c - last + k

        @pl.when(receives(right) & (k >= position(right)))
        def _():
            def step(rows):
                part[shard, p, rows, :] = (
                    part[shard, p, rows, :].astype(F32) + came[shard, p, rows, :].astype(F32)
                ).astype(BF16)

            over_rows(step)

    def start_index(right, index):
        if parts <= index < n_col * parts:
            start_out(right, index // parts, index % parts)

    def line_step(k, p):
        index = k * parts + p
        for right in (True, False):
            take_in(right, k, p)
            if ahead < parts:
                start_index(right, index + ahead)
            add_in(right, k, p)
            if ahead >= parts:
                start_index(right, index + ahead)
        if k == n_col - 2:
            pl.when(has_right)(lambda: add_products(1, me_c + 1, p))
            pl.when(has_left)(lambda: add_products(2, me_c - 1, p))

    def message_copy(right):
        slot = 0 if right else 1
        return push(
            message.at[slot], message_in.at[slot], msg_send.at[slot], msg_recv.at[slot],
            "col", me_c + 1 if right else me_c - 1,
        )

    def send_messages():
        for right in (True, False):
            slot = 0 if right else 1

            @pl.when(sends(right))
            def _():
                row = as_row(jnp.sum(prods[slot + 1], axis=1, keepdims=True))
                message[slot] = jnp.broadcast_to(row, (8, LANES))
                message_copy(right).start()

    def pr_copy(k):
        return push(
            prods_out, prods_in.at[me_r], pr_send.at[k], pr_recv.at[me_r],
            "row", lax.rem(me_r + k, n_row),
        )

    def send_products():
        row = as_row(jnp.sum(prods[0], axis=1, keepdims=True))
        prods_out[...] = jnp.broadcast_to(row, (8, LANES))
        for right in (True, False):
            slot = 0 if right else 1

            @pl.when(receives(right))
            def _():
                arrive(message_in.at[slot], msg_recv.at[slot])
                prods_out[...] += message_in[slot]

        for k in range(1, n_row):
            pr_copy(k).start()

    def take_products():
        summed = prods_out[...]
        for k in range(1, n_row):
            peer = lax.rem(me_r + k, n_row)
            arrive(prods_in.at[peer], pr_recv.at[peer])
            summed = summed + prods_in[peer]
        column = as_column(summed[:1], tokens)
        inverse = scales[me_c]
        scale[...] = inverse * inverse * inverse * (column / full)

    def weight(p):
        left = mid_all[:, p].reshape(n_col * tokens, fc)
        rows = pl.ds(p * fc, fc)
        factor = gain_column[rows, :]
        for at in range(0, depth, block):
            value = lax.dot_general(
                left, scaled[:, at : at + block], (((0,), (0,)), ((), ())),
                preferred_element_type=F32,
            )
            for b in range(0, block, LANES):
                grad_w[rows, at + b : at + b + LANES] = (value[:, b : b + LANES] * factor).astype(BF16)

    def term_copy(to, p):
        return push(
            term.at[p], later.at[me_s, p], term_send.at[to, p], term_recv.at[me_s, p],
            "section", to,
        )

    def finish(p):
        def step(rows):
            value = (
                part[me_c, p, rows, :].astype(F32)
                + from_left[me_c, p, rows, :].astype(F32)
                + from_right[me_c, p, rows, :].astype(F32)
            ) * gain[:, cols(p)]
            own = (
                scales[me_c, rows, :][:, :1] * value
                - mid_all[me_c, p, rows, :].astype(F32) * scale[rows, :][:, :1]
            )
            term[p, rows, :] = own.astype(BF16)
            total[p, rows, :] = top[rows, cols(p)].astype(F32) + own

        over_rows(step)
        for to in range(n_sec - 1):
            pl.when(me_s > to)(lambda: term_copy(to, p).start())

    def conclude(p):
        for source in range(1, n_sec):
            @pl.when(me_s < source)
            def _():
                arrive(later.at[source, p], term_recv.at[source, p])

                def step(rows):
                    total[p, rows, :] += later[source, p, rows, :].astype(F32)

                over_rows(step)

        def step(rows):
            res[rows, cols(p)] = total[p, rows, :].astype(BF16)

        over_rows(step)

    query_in.wait()

    def own_lap(p, _):
        w_copy(p).wait()
        product(
            me_r * subs, subs, lambda: query_all[own_query].reshape(subs * tokens, depth), p
        )
        return 0

    lax.fori_loop(0, parts, own_lap, 0)
    gain_in.wait()
    blocks = width // LANES
    lax.fori_loop(0, blocks // 2, turn_gain, 0)
    if n_row > 1 and subs > 1:
        x_next(0)
    lax.fori_loop(blocks // 2, blocks, turn_gain, 0)

    for p in range(parts):
        mid_in(p).wait()
    square(me_c)
    prods[...] = jnp.zeros(prods.shape, F32)

    @pl.when(jnp.logical_not(has_left))
    def _():
        from_left[me_c] = jnp.zeros(from_left.shape[1:], BF16)

    @pl.when(jnp.logical_not(has_right))
    def _():
        from_right[me_c] = jnp.zeros(from_right.shape[1:], BF16)

    steps = [(k, at) for k in range(1, n_row) for at in range(subs)]
    held = steps[-1:] if subs > 1 and n_col > 2 else []
    steps = steps[: len(steps) - len(held)]
    for k, at in steps[:-1]:
        x_arrive(k, at)
        for p in range(parts):
            x_product(k, at, p)
        if k == 1 and 0 < at < subs - 1:
            x_next(at)
    for p in range(parts):
        for k, at in steps[-1:]:
            if p == 0:
                x_arrive(k, at)
            x_product(k, at, p)
        if n_col > 1:
            line_step(0, p)
    for p in range(parts):
        if n_col < 3:
            add_products(0, me_c, p)
    for k in range(1, last):
        for p in range(parts):
            for far, at in held if k == 1 else []:
                if p == 0:
                    x_arrive(far, at)
                x_product(far, at, p)
            line_step(k, p)
            if k == 1:
                add_products(0, me_c, p)
            if p == 0:
                around(k, square)
            if p == parts // 2:
                if k == 1:
                    scale_query(me_c)
                else:
                    around(k - 1, scale_query)
    if n_col > 1:
        send_messages()
        around(last, square)
        if last > 1:
            around(last - 1, scale_query)
        else:
            scale_query(me_c)
        around(last, scale_query)
    else:
        scale_query(me_c)
    top_in.wait()
    done = 0
    for p in range(parts):
        weight(p)
        if n_col > 1:
            line_step(last, p)
        if p == parts // 4:
            send_products()
        if p == parts // 2:
            take_products()
        if p >= parts // 2:
            while done <= p:
                finish(done)
                if done:
                    conclude(done - 1)
                done += 1
    conclude(parts - 1)

    for right in (True, False):
        for k in range(n_row - 1):
            @pl.when(x_sends(k, right))
            def _():
                for at in range(subs - 1 if k == 0 else 0, subs):
                    x_send(k, sub_of(at, right), right).wait_send()

        @pl.when(sends(right))
        def _():
            send = right_send if right else left_send
            for k in range(n_col):
                for p in range(parts):
                    arrive(part.at[0, p], send.at[k, p])
            message_copy(right).wait_send()
    for k in range(1, n_row):
        for shard in range(n_col):
            sq_copy(k, shard).wait_send()
        pr_copy(k).wait_send()
    for to in range(n_sec - 1):
        @pl.when(me_s > to)
        def _():
            for p in range(parts):
                term_copy(to, p).wait_send()


def write_out(pieces, grad_w, res, grad_out, res_out, sem):
    tall = grad_w.shape[0] // pieces
    copies = [
        pltpu.make_async_copy(
            grad_w.at[pl.ds(i * tall, tall)], grad_out.at[pl.ds(i * tall, tall)], sem.at[i]
        )
        for i in range(pieces)
    ]
    copies.append(pltpu.make_async_copy(res, res_out, sem.at[pieces]))
    for copy in copies:
        copy.start()
    for copy in copies:
        copy.wait()


def body(mid, query_grad, top_grad, w_query, gain):
    n_sec, n_row, n_col = (lax.axis_size(a) for a in ("section", "row", "col"))
    tokens, width = mid.shape[1:]
    rows, depth = query_grad.shape[1:]
    subs = rows // tokens
    parts = PIECES
    fc = width // parts
    hbm = pl.BlockSpec(memory_space=pltpu.HBM)
    anywhere = pl.BlockSpec(memory_space=pl.ANY)
    in_vmem = pl.BlockSpec(memory_space=pltpu.VMEM)
    dma = pltpu.SemaphoreType.DMA
    vmem = pltpu.VMEM
    grad_w, res = pl.pallas_call(
        functools.partial(kernel, n_sec, n_row, n_col, parts, AHEAD),
        out_shape=(vmem((width, depth), BF16), vmem((tokens, width), BF16)),
        in_specs=[hbm] * 5,
        out_specs=(in_vmem, in_vmem),
        scratch_shapes=[
            vmem((n_col, parts, tokens, fc), BF16),
            vmem((n_col, tokens, depth), BF16),
            vmem((n_col, parts, tokens, fc), BF16),
            vmem((n_col, parts, tokens, fc), BF16),
            vmem((n_col, parts, tokens, fc), BF16),
            vmem((n_col * tokens, depth), BF16),
            vmem((1, width), F32),
            vmem((width, LANES), F32),
            vmem((tokens, width), BF16),
            vmem((n_col, tokens, LANES), F32),
            vmem((n_row, n_col, tokens, LANES), F32),
            vmem((n_col, tokens, LANES), F32),
            vmem((tokens, LANES), F32),
            vmem((3, tokens, LANES), F32),
            vmem((2, 8, LANES), F32),
            vmem((2, 8, LANES), F32),
            vmem((8, LANES), F32),
            vmem((n_row, 8, LANES), F32),
            vmem((parts, tokens, fc), BF16),
            vmem((n_sec, parts, tokens, fc), BF16),
            vmem((parts, tokens, fc), F32),
            dma((parts,)), dma, dma, dma, dma((parts,)),
            dma((n_col,)), dma((n_col,)), dma((n_col,)),
            dma((n_col, parts)), dma((n_col, parts)),
            dma((n_col, parts)), dma((n_col, parts)),
            dma((n_row, n_col)), dma((n_row, n_col)),
            dma((2,)), dma((2,)), dma((n_row,)), dma((n_row,)),
            dma((n_sec, parts)), dma((n_sec, parts)),
        ],
        compiler_params=pltpu.CompilerParams(
            collective_id=0, has_side_effects=True, vmem_limit_bytes=40 * 1024 * 1024
        ),
    )(mid[0], query_grad[0].reshape(subs, tokens, depth), top_grad, gain, w_query[0])
    pieces = 8
    weight_grad, residual = pl.pallas_call(
        functools.partial(write_out, pieces),
        out_shape=(
            jax.ShapeDtypeStruct((width, depth), BF16),
            jax.ShapeDtypeStruct((tokens, width), BF16),
        ),
        in_specs=[anywhere] * 2,
        out_specs=(anywhere, anywhere),
        scratch_shapes=[dma((pieces + 1,))],
        compiler_params=pltpu.CompilerParams(vmem_limit_bytes=2 * 1024 * 1024),
    )(grad_w, res)
    return (weight_grad[None], residual[None])


def solution(mesh):
    return jax.shard_map(
        body,
        mesh=mesh,
        in_specs=(
            P("section", ("groups", "col"), "row"),
            P("section", ("groups", "row"), "col"),
            P(("groups", "col"), "row"),
            P("section", "row", "col"),
            P("section", "row"),
        ),
        out_specs=(P(("groups", "section"), "row", "col"), P("section", ("groups", "col"), "row")),
        check_vma=False,
    )
```

```python
import functools

import jax
import jax.numpy as jnp
from jax import lax
from jax.experimental import pallas as pl
from jax.experimental.pallas import tpu as pltpu
from jax.sharding import PartitionSpec as P

EPSILON = 1e-05
LANES = 128
ROWS = 16
PIECES = 4
AHEAD = 2
HALVES = 2
F32 = jnp.float32
BF16 = jnp.bfloat16
MESH = pl.DeviceIdType.MESH


def lane_sums(value):
    total = value[:, :LANES]
    for at in range(LANES, value.shape[1], LANES):
        total = total + value[:, at : at + LANES]
    return total


def diagonal(rows):
    shape = (rows, LANES)
    return lax.broadcasted_iota(jnp.int32, shape, 0) == lax.broadcasted_iota(jnp.int32, shape, 1)


def as_row(column):
    wide = jnp.broadcast_to(column, (column.shape[0], LANES))
    return jnp.sum(jnp.where(diagonal(column.shape[0]), wide, 0.0), axis=0, keepdims=True)


def as_column(row, rows):
    wide = jnp.broadcast_to(row, (rows, LANES))
    return jnp.sum(jnp.where(diagonal(rows), wide, 0.0), axis=1, keepdims=True)


def push(src, dst, send, recv, axis, peer):
    return pltpu.make_async_remote_copy(
        src_ref=src,
        dst_ref=dst,
        send_sem=send,
        recv_sem=recv,
        device_id={axis: peer},
        device_id_type=MESH,
    )


def arrive(ref, sem):
    pltpu.make_async_copy(ref, ref, sem).wait()


def kernel(
    n_sec, n_row, n_col, parts, ahead, halves,
    mid, query, top_hbm, gain_hbm, w_hbm,
    grad_w, res,
    mid_all, query_all, part, from_left, from_right, scaled, gain, gain_column, top,
    squares, squares_in, inverses, scales, scale,
    prods, message, message_in, prods_out, prods_in,
    term, later, total,
    mid_sem, query_sem, top_sem, gain_sem, w_sem,
    x_right, x_left, x_recv, right_send, right_recv, left_send, left_recv,
    sq_send, sq_recv, inv_right, inv_left, inv_recv, msg_send, msg_recv, pr_send, pr_recv, term_send, term_recv,
):
    me_s, me_r, me_c = (lax.axis_index(a) for a in ("section", "row", "col"))
    tokens, width = mid.shape
    subs, _, depth = query.shape
    fc = width // parts
    tile = min(1024, fc)
    block = min(512, depth)
    full = width * n_row
    last = n_col - 1
    has_left, has_right = me_c > 0, me_c < last

    def cols(p):
        return pl.ds(p * fc, fc)

    own_query = pl.ds(me_r * subs, subs)
    query_in = pltpu.make_async_copy(query, query_all.at[own_query], query_sem)
    gain_in = pltpu.make_async_copy(gain_hbm, gain, gain_sem)
    top_in = pltpu.make_async_copy(top_hbm, top, top_sem)

    def mid_in(p):
        return pltpu.make_async_copy(mid.at[:, cols(p)], mid_all.at[me_c, p], mid_sem.at[p])

    def w_copy(p):
        rows = pl.ds(pl.multiple_of(p * fc, fc), fc)
        return pltpu.make_async_copy(w_hbm.at[rows], grad_w.at[rows], w_sem.at[p])

    barrier = pltpu.get_barrier_semaphore()

    def greet(axis, peer):
        pl.semaphore_signal(barrier, inc=1, device_id={axis: peer}, device_id_type=MESH)

    for k in range(1, n_row):
        greet("row", lax.rem(me_r + k, n_row))
    pl.when(has_left)(lambda: greet("col", me_c - 1))
    pl.when(has_right)(lambda: greet("col", me_c + 1))
    for k in range(1, n_sec):
        greet("section", lax.rem(me_s + k, n_sec))
    query_in.start()
    gain_in.start()
    for p in range(parts):
        w_copy(p).start()
    for p in range(parts):
        mid_in(p).start()
    top_in.start()
    beside = (me_c + n_col - 1) // n_col + (2 * n_col - 2 - me_c) // n_col
    pl.semaphore_wait(barrier, n_row - 1 + n_sec - 1 + beside)

    def position(right):
        return me_c if right else last - me_c

    def sends(right):
        return has_right if right else has_left

    def receives(right):
        return has_left if right else has_right

    def line(src, dst, right, k, p):
        send, recv = (right_send, right_recv) if right else (left_send, left_recv)
        return push(
            src, dst, send.at[k, p], recv.at[k, p], "col", me_c + 1 if right else me_c - 1
        )

    def mid_copy(right, k, p):
        shard = me_c - k if right else me_c + k
        src = mid.at[:, cols(p)] if k == 0 else mid_all.at[shard, p]
        return line(src, mid_all.at[shard, p], right, k, p)

    def sum_copy(right, k, p):
        shard = me_c + n_col - k if right else me_c - n_col + k
        came = from_left if right else from_right
        return line(part.at[shard, p], came.at[shard, p], right, k, p)

    def start_out(right, k, p):
        if k == 0:
            pl.when(sends(right))(lambda: mid_copy(right, k, p).start())
            return
        early = k <= position(right)
        pl.when(sends(right) & early)(lambda: mid_copy(right, k, p).start())
        pl.when(sends(right) & jnp.logical_not(early))(lambda: sum_copy(right, k, p).start())

    for p in range(parts):
        for right in (True, False):
            start_out(right, 0, p)

    def x_send(k, sub, right):
        piece = me_r - k if right else me_r + k
        shard = piece * subs + sub
        src = query.at[sub] if k == 0 else query_all.at[shard]
        return push(
            src, query_all.at[shard], (x_right if right else x_left).at[shard], x_recv.at[shard],
            "row", me_r + 1 if right else me_r - 1,
        )

    def x_sends(k, right):
        if right:
            return (me_r - k >= 0) & (me_r < n_row - 1)
        return (me_r + k < n_row) & (me_r > 0)

    def sub_of(at, right):
        return at if right else subs - 1 - at

    for right in (True, False):
        pl.when(x_sends(0, right))(lambda: x_send(0, sub_of(0, right), right).start())

    def product(shard, count, load, p):
        for t in range(fc // tile):
            rows = pl.ds(pl.multiple_of(p * fc + t * tile, tile), tile)
            value = lax.dot_general(
                load(), grad_w[rows, :], (((1,), (1,)), ((), ())), preferred_element_type=F32
            ).astype(BF16)
            for at in range(count):
                part[shard + at, p, :, t * tile : (t + 1) * tile] = value[
                    at * tokens : (at + 1) * tokens
                ]

    def over_rows(step, count=tokens // ROWS):
        def lap(i, _):
            step(pl.ds(pl.multiple_of(i * ROWS, ROWS), ROWS))
            return 0

        lax.fori_loop(0, count, lap, 0)

    def sq_copy(k):
        return push(
            squares, squares_in.at[me_r], sq_send.at[k], sq_recv.at[me_r],
            "row", lax.rem(me_r + k, n_row),
        )

    def square():
        def step(rows):
            summed = jnp.zeros((ROWS, LANES), F32)
            for p in range(parts):
                value = mid_all[me_c, p, rows, :].astype(F32)
                summed = summed + lane_sums(value * value)
            prods[0, rows, :] = summed

        over_rows(step)
        row = as_row(jnp.sum(prods[0], axis=1, keepdims=True))
        squares[...] = jnp.broadcast_to(row, (8, LANES))
        for k in range(1, n_row):
            sq_copy(k).start()

    def inverse_copy(right, k):
        shard = me_c - k if right else me_c + k
        row = inverses.at[shard]
        return push(
            row, row, (inv_right if right else inv_left).at[shard], inv_recv.at[shard],
            "col", me_c + 1 if right else me_c - 1,
        )

    def inverse_sends(right, k):
        return (k <= position(right)) & sends(right)

    def own_inverse():
        summed = squares[...]
        for k in range(1, n_row):
            peer = lax.rem(me_r + k, n_row)
            arrive(squares_in.at[peer], sq_recv.at[peer])
            summed = summed + squares_in[peer]
        inverses[me_c] = lax.rsqrt(summed / full + EPSILON)
        for right in (True, False):
            pl.when(inverse_sends(right, 0))(lambda: inverse_copy(right, 0).start())

    def pass_inverses(k):
        for right in (True, False):
            shard = me_c - k if right else me_c + k

            @pl.when((shard >= 0) if right else (shard < n_col))
            def _():
                arrive(inverses.at[shard], inv_recv.at[shard])
                if k < last:
                    pl.when(inverse_sends(right, k))(lambda: inverse_copy(right, k).start())

    def scale_query(shard):
        column = as_column(inverses[shard, :1, :], tokens)
        scales[shard] = jnp.broadcast_to(column, (tokens, LANES))

        def lap(i, _):
            rows = pl.ds(pl.multiple_of(i * ROWS, ROWS), ROWS)
            factor = scales[shard, rows, :][:, :1] * (n_col * tokens) ** -0.5
            at = pl.ds(pl.multiple_of(shard * tokens + i * ROWS, ROWS), ROWS)
            scaled[at, :] = (query_all[shard, rows, :].astype(F32) * factor).astype(BF16)
            return 0

        lax.fori_loop(0, tokens // ROWS, lap, 0)

    def scale_at(k):
        if k == 0:
            scale_query(me_c)
            return
        pl.when(me_c - k >= 0)(lambda: scale_query(me_c - k))
        pl.when(me_c + k < n_col)(lambda: scale_query(me_c + k))

    def x_next(at):
        for right in (True, False):
            @pl.when(x_sends(0, right))
            def _():
                x_send(0, sub_of(at, right), right).wait_send()
                x_send(0, sub_of(at + 1, right), right).start()

    def x_shards(k, at):
        for right in (True, False):
            piece = me_r - k if right else me_r + k
            sub = sub_of(at, right)
            yield right, piece * subs + sub, sub, (piece >= 0) if right else (piece < n_row)

    def x_arrive(k, at):
        for right, shard, sub, valid in x_shards(k, at):
            @pl.when(valid)
            def _():
                arrive(query_all.at[shard], x_recv.at[shard])
                if k < n_row - 1:
                    pl.when(x_sends(k, right))(lambda: x_send(k, sub, right).start())

    def x_product(k, at, p):
        for _, shard, _, valid in x_shards(k, at):
            pl.when(valid)(lambda: product(shard, 1, lambda: query_all[shard], p))

    def turn_gain(b, _):
        at = pl.ds(pl.multiple_of(b * LANES, LANES), LANES)
        column = as_column(gain[:, at], LANES)
        gain_column[at, :] = jnp.broadcast_to(column, (LANES, LANES))
        return 0

    def add_products(slot, shard, p):
        def step(rows):
            value = part[shard, p, rows, :].astype(F32) * gain[:, cols(p)]
            prods[slot, rows, :] += lane_sums(mid_all[shard, p, rows, :].astype(F32) * value)

        over_rows(step)

    def take_in(right, k, p):
        came = from_left if right else from_right
        recv = right_recv if right else left_recv
        pl.when(receives(right))(lambda: arrive(came.at[0, p], recv.at[k, p]))

    def add_in(right, k, p):
        if k == last:
            return
        came = from_left if right else from_right
        shard = me_c + last - k if right else me_c - last + k

        @pl.when(receives(right) & (k >= position(right)))
        def _():
            def step(rows):
                part[shard, p, rows, :] = (
                    part[shard, p, rows, :].astype(F32) + came[shard, p, rows, :].astype(F32)
                ).astype(BF16)

            over_rows(step)

    def start_index(right, index):
        if parts <= index < n_col * parts:
            start_out(right, index // parts, index % parts)

    def line_step(k, p):
        index = k * parts + p
        for right in (True, False):
            take_in(right, k, p)
            if ahead < parts:
                start_index(right, index + ahead)
            add_in(right, k, p)
            if ahead >= parts:
                start_index(right, index + ahead)
        if k == n_col - 2:
            pl.when(has_right)(lambda: add_products(1, me_c + 1, p))
            pl.when(has_left)(lambda: add_products(2, me_c - 1, p))

    def message_copy(right):
        slot = 0 if right else 1
        return push(
            message.at[slot], message_in.at[slot], msg_send.at[slot], msg_recv.at[slot],
            "col", me_c + 1 if right else me_c - 1,
        )

    def send_messages():
        for right in (True, False):
            slot = 0 if right else 1

            @pl.when(sends(right))
            def _():
                row = as_row(jnp.sum(prods[slot + 1], axis=1, keepdims=True))
                message[slot] = jnp.broadcast_to(row, (8, LANES))
                message_copy(right).start()

    def pr_copy(k):
        return push(
            prods_out, prods_in.at[me_r], pr_send.at[k], pr_recv.at[me_r],
            "row", lax.rem(me_r + k, n_row),
        )

    def send_products():
        row = as_row(jnp.sum(prods[0], axis=1, keepdims=True))
        prods_out[...] = jnp.broadcast_to(row, (8, LANES))
        for right in (True, False):
            slot = 0 if right else 1

            @pl.when(receives(right))
            def _():
                arrive(message_in.at[slot], msg_recv.at[slot])
                prods_out[...] += message_in[slot]

        for k in range(1, n_row):
            pr_copy(k).start()

    def take_products():
        summed = prods_out[...]
        for k in range(1, n_row):
            peer = lax.rem(me_r + k, n_row)
            arrive(prods_in.at[peer], pr_recv.at[peer])
            summed = summed + prods_in[peer]
        column = as_column(summed[:1], tokens)
        inverse = scales[me_c]
        scale[...] = inverse * inverse * inverse * (column / full)

    def weight(p):
        left = mid_all[:, p].reshape(n_col * tokens, fc)
        rows = pl.ds(p * fc, fc)
        factor = gain_column[rows, :]
        for at in range(0, depth, block):
            value = lax.dot_general(
                left, scaled[:, at : at + block], (((0,), (0,)), ((), ())),
                preferred_element_type=F32,
            )
            for b in range(0, block, LANES):
                grad_w[rows, at + b : at + b + LANES] = (value[:, b : b + LANES] * factor).astype(BF16)

    half = tokens // halves

    def term_copy(to, p, h):
        rows = pl.ds(h * half, half)
        return push(
            term.at[p, rows], later.at[me_s, p, rows], term_send.at[to, p, h],
            term_recv.at[me_s, p, h], "section", to,
        )

    def over_half(h, step):
        def lap(i, _):
            step(pl.ds(pl.multiple_of(h * half + i * ROWS, ROWS), ROWS))
            return 0

        lax.fori_loop(0, half // ROWS, lap, 0)

    def finish(p):
        def step(rows):
            value = (
                part[me_c, p, rows, :].astype(F32)
                + from_left[me_c, p, rows, :].astype(F32)
                + from_right[me_c, p, rows, :].astype(F32)
            ) * gain[:, cols(p)]
            own = (
                scales[me_c, rows, :][:, :1] * value
                - mid_all[me_c, p, rows, :].astype(F32) * scale[rows, :][:, :1]
            )
            term[p, rows, :] = own.astype(BF16)
            total[p, rows, :] = top[rows, cols(p)].astype(F32) + own

        for h in range(halves):
            over_half(h, step)
            for to in range(n_sec - 1):
                pl.when(me_s > to)(lambda: term_copy(to, p, h).start())

    def no_later():
        for source in range(1, n_sec):
            @pl.when(me_s >= source)
            def _():
                later[source] = jnp.zeros(later.shape[1:], BF16)

    def conclude(p):
        def step(rows):
            value = total[p, rows, :]
            for source in range(1, n_sec):
                value = value + later[source, p, rows, :].astype(F32)
            res[rows, cols(p)] = value.astype(BF16)

        for h in range(halves):
            for source in range(1, n_sec):
                @pl.when(me_s < source)
                def _():
                    rows = pl.ds(h * half, half)
                    arrive(later.at[source, p, rows], term_recv.at[source, p, h])

            over_half(h, step)

    def line_waits(right, slots):
        send = right_send if right else left_send
        for k in slots:
            for p in range(parts):
                arrive(part.at[0, p], send.at[k, p])

    def early_waits():
        for right in (True, False):
            for k in range(n_row - 1):
                @pl.when(x_sends(k, right))
                def _():
                    for at in range(subs - 1 if k == 0 else 0, subs):
                        x_send(k, sub_of(at, right), right).wait_send()

            pl.when(sends(right))(lambda: line_waits(right, range(last)))
            for k in range(last):
                pl.when(inverse_sends(right, k))(lambda: inverse_copy(right, k).wait_send())
        for k in range(1, n_row):
            sq_copy(k).wait_send()
            pr_copy(k).wait_send()

    def late_waits():
        for right in (True, False):
            @pl.when(sends(right))
            def _():
                line_waits(right, [last])
                message_copy(right).wait_send()
        for to in range(n_sec - 1):
            @pl.when(me_s > to)
            def _():
                for p in range(parts):
                    for h in range(halves):
                        term_copy(to, p, h).wait_send()

    query_in.wait()

    def own_lap(p, _):
        w_copy(p).wait()
        product(
            me_r * subs, subs, lambda: query_all[own_query].reshape(subs * tokens, depth), p
        )
        return 0

    lax.fori_loop(0, parts, own_lap, 0)
    for p in range(parts):
        mid_in(p).wait()
    square()
    gain_in.wait()
    blocks = width // LANES
    lax.fori_loop(0, blocks // 2, turn_gain, 0)
    if n_row > 1 and subs > 1:
        x_next(0)
    lax.fori_loop(blocks // 2, blocks, turn_gain, 0)

    @pl.when(jnp.logical_not(has_left))
    def _():
        from_left[me_c] = jnp.zeros(from_left.shape[1:], BF16)

    @pl.when(jnp.logical_not(has_right))
    def _():
        from_right[me_c] = jnp.zeros(from_right.shape[1:], BF16)

    steps = [(k, at) for k in range(1, n_row) for at in range(subs)]
    held = steps[-1:] if subs > 1 and n_col > 2 else []
    steps = steps[: len(steps) - len(held)]
    for k, at in steps[:-1]:
        x_arrive(k, at)
        for p in range(parts):
            x_product(k, at, p)
        if k == 1 and 0 < at < subs - 1:
            x_next(at)
    for p in range(parts):
        for k, at in steps[-1:]:
            if p == 0:
                x_arrive(k, at)
            x_product(k, at, p)
        if p == 0:
            prods[...] = jnp.zeros(prods.shape, F32)
        if n_col > 1:
            line_step(0, p)
        if p == min(1, parts - 1):
            own_inverse()
    if n_col > 1:
        pass_inverses(1)
    if n_col < 3:
        for p in range(parts):
            add_products(0, me_c, p)
    for k in range(1, last):
        for p in range(parts):
            for far, at in held if k == 1 else []:
                if p == 0:
                    x_arrive(far, at)
                x_product(far, at, p)
            line_step(k, p)
            if k == 1:
                add_products(0, me_c, p)
            if p == (1 if k == 1 and last > 2 else 0):
                pass_inverses(k + 1)
                if k == 1:
                    scale_at(0)
                scale_at(k)
                if k == last - 1:
                    scale_at(last)
            if k == last - 1:
                if p == parts - 1:
                    send_messages()
                weight(p)
    if 1 < n_col < 3:
        send_messages()
    if n_col < 3:
        for k in range(n_col):
            scale_at(k)
        for p in range(parts):
            weight(p)
    top_in.wait()
    no_later()
    done = 0
    for p in range(parts):
        if n_col > 1:
            line_step(last, p)
        if p == parts // 4:
            send_products()
        if p == parts // 2:
            take_products()
        if p >= parts // 2:
            while done <= p:
                finish(done)
                if done:
                    conclude(done - 1)
                done += 1
        if p == parts - 2:
            early_waits()
    if parts == 1:
        early_waits()
    conclude(parts - 1)
    late_waits()


def write_out(pieces, grad_w, res, grad_out, res_out, sem):
    tall = grad_w.shape[0] // pieces
    copies = [
        pltpu.make_async_copy(
            grad_w.at[pl.ds(i * tall, tall)], grad_out.at[pl.ds(i * tall, tall)], sem.at[i]
        )
        for i in range(pieces)
    ]
    copies.append(pltpu.make_async_copy(res, res_out, sem.at[pieces]))
    for copy in copies:
        copy.start()
    for copy in copies:
        copy.wait()


def body(mid, query_grad, top_grad, w_query, gain):
    n_sec, n_row, n_col = (lax.axis_size(a) for a in ("section", "row", "col"))
    tokens, width = mid.shape[1:]
    rows, depth = query_grad.shape[1:]
    subs = rows // tokens
    parts = PIECES
    fc = width // parts
    hbm = pl.BlockSpec(memory_space=pltpu.HBM)
    anywhere = pl.BlockSpec(memory_space=pl.ANY)
    in_vmem = pl.BlockSpec(memory_space=pltpu.VMEM)
    dma = pltpu.SemaphoreType.DMA
    vmem = pltpu.VMEM
    grad_w, res = pl.pallas_call(
        functools.partial(kernel, n_sec, n_row, n_col, parts, AHEAD, HALVES),
        out_shape=(vmem((width, depth), BF16), vmem((tokens, width), BF16)),
        in_specs=[hbm] * 5,
        out_specs=(in_vmem, in_vmem),
        scratch_shapes=[
            vmem((n_col, parts, tokens, fc), BF16),
            vmem((n_col, tokens, depth), BF16),
            vmem((n_col, parts, tokens, fc), BF16),
            vmem((n_col, parts, tokens, fc), BF16),
            vmem((n_col, parts, tokens, fc), BF16),
            vmem((n_col * tokens, depth), BF16),
            vmem((1, width), F32),
            vmem((width, LANES), F32),
            vmem((tokens, width), BF16),
            vmem((8, LANES), F32),
            vmem((n_row, 8, LANES), F32),
            vmem((n_col, 8, LANES), F32),
            vmem((n_col, tokens, LANES), F32),
            vmem((tokens, LANES), F32),
            vmem((3, tokens, LANES), F32),
            vmem((2, 8, LANES), F32),
            vmem((2, 8, LANES), F32),
            vmem((8, LANES), F32),
            vmem((n_row, 8, LANES), F32),
            vmem((parts, tokens, fc), BF16),
            vmem((n_sec, parts, tokens, fc), BF16),
            vmem((parts, tokens, fc), F32),
            dma((parts,)), dma, dma, dma, dma((parts,)),
            dma((n_col,)), dma((n_col,)), dma((n_col,)),
            dma((n_col, parts)), dma((n_col, parts)),
            dma((n_col, parts)), dma((n_col, parts)),
            dma((n_row,)), dma((n_row,)), dma((n_col,)), dma((n_col,)), dma((n_col,)),
            dma((2,)), dma((2,)), dma((n_row,)), dma((n_row,)),
            dma((n_sec, parts, HALVES)), dma((n_sec, parts, HALVES)),
        ],
        compiler_params=pltpu.CompilerParams(
            collective_id=0, has_side_effects=True, vmem_limit_bytes=40 * 1024 * 1024
        ),
    )(mid[0], query_grad[0].reshape(subs, tokens, depth), top_grad, gain, w_query[0])
    pieces = 8
    weight_grad, residual = pl.pallas_call(
        functools.partial(write_out, pieces),
        out_shape=(
            jax.ShapeDtypeStruct((width, depth), BF16),
            jax.ShapeDtypeStruct((tokens, width), BF16),
        ),
        in_specs=[anywhere] * 2,
        out_specs=(anywhere, anywhere),
        scratch_shapes=[dma((pieces + 1,))],
        compiler_params=pltpu.CompilerParams(vmem_limit_bytes=2 * 1024 * 1024),
    )(grad_w, res)
    return (weight_grad[None], residual[None])


def solution(mesh):
    return jax.shard_map(
        body,
        mesh=mesh,
        in_specs=(
            P("section", ("groups", "col"), "row"),
            P("section", ("groups", "row"), "col"),
            P(("groups", "col"), "row"),
            P("section", "row", "col"),
            P("section", "row"),
        ),
        out_specs=(P(("groups", "section"), "row", "col"), P("section", ("groups", "col"), "row")),
        check_vma=False,
    )
```

```python
import functools

import jax
import jax.numpy as jnp
from jax import lax
from jax.experimental import pallas as pl
from jax.experimental.pallas import tpu as pltpu
from jax.sharding import PartitionSpec as P

EPSILON = 1e-05
LANES = 128
ROWS = 16
PIECES = 4
AHEAD = 2
HALVES = 2
F32 = jnp.float32
BF16 = jnp.bfloat16
MESH = pl.DeviceIdType.MESH


def lane_sums(value):
    total = value[:, :LANES]
    for at in range(LANES, value.shape[1], LANES):
        total = total + value[:, at : at + LANES]
    return total


def diagonal(rows):
    shape = (rows, LANES)
    return lax.broadcasted_iota(jnp.int32, shape, 0) == lax.broadcasted_iota(jnp.int32, shape, 1)


def as_row(column):
    wide = jnp.broadcast_to(column, (column.shape[0], LANES))
    return jnp.sum(jnp.where(diagonal(column.shape[0]), wide, 0.0), axis=0, keepdims=True)


def as_column(row, rows):
    wide = jnp.broadcast_to(row, (rows, LANES))
    return jnp.sum(jnp.where(diagonal(rows), wide, 0.0), axis=1, keepdims=True)


def push(src, dst, send, recv, axis, peer):
    return pltpu.make_async_remote_copy(
        src_ref=src,
        dst_ref=dst,
        send_sem=send,
        recv_sem=recv,
        device_id={axis: peer},
        device_id_type=MESH,
    )


def arrive(ref, sem):
    pltpu.make_async_copy(ref, ref, sem).wait()


def kernel(
    n_sec, n_row, n_col, parts, ahead, halves,
    mid, query, top_hbm, gain_hbm, w_hbm,
    grad_w, res,
    mid_all, query_all, part, from_left, from_right, scaled, gain, gain_column, top,
    squares, squares_in, inverses, scales, scale,
    prods, message, message_in, prods_out, prods_in,
    term, later, total,
    mid_sem, query_sem, top_sem, gain_sem, w_sem,
    x_right, x_left, x_recv, right_send, right_recv, left_send, left_recv,
    sq_send, sq_recv, inv_right, inv_left, inv_recv, msg_send, msg_recv, pr_send, pr_recv, term_send, term_recv,
):
    me_s, me_r, me_c = (lax.axis_index(a) for a in ("section", "row", "col"))
    tokens, width = mid.shape
    subs, _, depth = query.shape
    fc = width // parts
    tile = min(1024, fc)
    block = min(512, depth)
    full = width * n_row
    last = n_col - 1
    has_left, has_right = me_c > 0, me_c < last

    def cols(p):
        return pl.ds(p * fc, fc)

    own_query = pl.ds(me_r * subs, subs)
    query_in = pltpu.make_async_copy(query, query_all.at[own_query], query_sem)
    gain_in = pltpu.make_async_copy(gain_hbm, gain, gain_sem)
    top_in = pltpu.make_async_copy(top_hbm, top, top_sem)

    def mid_in(p):
        return pltpu.make_async_copy(mid.at[:, cols(p)], mid_all.at[me_c, p], mid_sem.at[p])

    def w_copy(p):
        rows = pl.ds(pl.multiple_of(p * fc, fc), fc)
        return pltpu.make_async_copy(w_hbm.at[rows], grad_w.at[rows], w_sem.at[p])

    barrier = pltpu.get_barrier_semaphore()

    def greet(axis, peer):
        pl.semaphore_signal(barrier, inc=1, device_id={axis: peer}, device_id_type=MESH)

    for k in range(1, n_row):
        greet("row", lax.rem(me_r + k, n_row))
    pl.when(has_left)(lambda: greet("col", me_c - 1))
    pl.when(has_right)(lambda: greet("col", me_c + 1))
    for k in range(1, n_sec):
        greet("section", lax.rem(me_s + k, n_sec))
    query_in.start()
    gain_in.start()
    for p in range(parts):
        w_copy(p).start()
    for p in range(parts):
        mid_in(p).start()
    top_in.start()
    beside = (me_c + n_col - 1) // n_col + (2 * n_col - 2 - me_c) // n_col
    pl.semaphore_wait(barrier, n_row - 1 + n_sec - 1 + beside)

    def position(right):
        return me_c if right else last - me_c

    def sends(right):
        return has_right if right else has_left

    def receives(right):
        return has_left if right else has_right

    def line(src, dst, right, k, p):
        send, recv = (right_send, right_recv) if right else (left_send, left_recv)
        return push(
            src, dst, send.at[k, p], recv.at[k, p], "col", me_c + 1 if right else me_c - 1
        )

    def mid_copy(right, k, p):
        shard = me_c - k if right else me_c + k
        src = mid.at[:, cols(p)] if k == 0 else mid_all.at[shard, p]
        return line(src, mid_all.at[shard, p], right, k, p)

    def sum_copy(right, k, p):
        shard = me_c + n_col - k if right else me_c - n_col + k
        came = from_left if right else from_right
        return line(part.at[shard, p], came.at[shard, p], right, k, p)

    def start_out(right, k, p):
        if k == 0:
            pl.when(sends(right))(lambda: mid_copy(right, k, p).start())
            return
        early = k <= position(right)
        pl.when(sends(right) & early)(lambda: mid_copy(right, k, p).start())
        pl.when(sends(right) & jnp.logical_not(early))(lambda: sum_copy(right, k, p).start())

    for p in range(parts):
        for right in (True, False):
            start_out(right, 0, p)

    def x_send(k, sub, right):
        piece = me_r - k if right else me_r + k
        shard = piece * subs + sub
        src = query.at[sub] if k == 0 else query_all.at[shard]
        return push(
            src, query_all.at[shard], (x_right if right else x_left).at[shard], x_recv.at[shard],
            "row", me_r + 1 if right else me_r - 1,
        )

    def x_sends(k, right):
        if right:
            return (me_r - k >= 0) & (me_r < n_row - 1)
        return (me_r + k < n_row) & (me_r > 0)

    def sub_of(at, right):
        return at if right else subs - 1 - at

    for right in (True, False):
        pl.when(x_sends(0, right))(lambda: x_send(0, sub_of(0, right), right).start())

    def product(shard, count, load, p):
        for t in range(fc // tile):
            rows = pl.ds(pl.multiple_of(p * fc + t * tile, tile), tile)
            value = lax.dot_general(
                load(), grad_w[rows, :], (((1,), (1,)), ((), ())), preferred_element_type=F32
            ).astype(BF16)
            for at in range(count):
                part[shard + at, p, :, t * tile : (t + 1) * tile] = value[
                    at * tokens : (at + 1) * tokens
                ]

    def over_rows(step, count=tokens // ROWS):
        def lap(i, _):
            step(pl.ds(pl.multiple_of(i * ROWS, ROWS), ROWS))
            return 0

        lax.fori_loop(0, count, lap, 0)

    def sq_copy(k):
        return push(
            squares, squares_in.at[me_r], sq_send.at[k], sq_recv.at[me_r],
            "row", lax.rem(me_r + k, n_row),
        )

    def square():
        def step(rows):
            summed = jnp.zeros((ROWS, LANES), F32)
            for p in range(parts):
                value = mid_all[me_c, p, rows, :].astype(F32)
                summed = summed + lane_sums(value * value)
            prods[0, rows, :] = summed

        over_rows(step)
        row = as_row(jnp.sum(prods[0], axis=1, keepdims=True))
        squares[...] = jnp.broadcast_to(row, (8, LANES))
        for k in range(1, n_row):
            sq_copy(k).start()

    def inverse_copy(right, k):
        shard = me_c - k if right else me_c + k
        row = inverses.at[shard]
        return push(
            row, row, (inv_right if right else inv_left).at[shard], inv_recv.at[shard],
            "col", me_c + 1 if right else me_c - 1,
        )

    def inverse_sends(right, k):
        return (k <= position(right)) & sends(right)

    def own_inverse():
        summed = squares[...]
        for k in range(1, n_row):
            peer = lax.rem(me_r + k, n_row)
            arrive(squares_in.at[peer], sq_recv.at[peer])
            summed = summed + squares_in[peer]
        inverses[me_c] = lax.rsqrt(summed / full + EPSILON)
        for right in (True, False):
            pl.when(inverse_sends(right, 0))(lambda: inverse_copy(right, 0).start())

    def pass_inverses(k):
        for right in (True, False):
            shard = me_c - k if right else me_c + k

            @pl.when((shard >= 0) if right else (shard < n_col))
            def _():
                arrive(inverses.at[shard], inv_recv.at[shard])
                if k < last:
                    pl.when(inverse_sends(right, k))(lambda: inverse_copy(right, k).start())

    def scale_query(shard):
        column = as_column(inverses[shard, :1, :], tokens)
        scales[shard] = jnp.broadcast_to(column, (tokens, LANES))

        def lap(i, _):
            rows = pl.ds(pl.multiple_of(i * ROWS, ROWS), ROWS)
            factor = scales[shard, rows, :][:, :1] * (n_col * tokens) ** -0.5
            at = pl.ds(pl.multiple_of(shard * tokens + i * ROWS, ROWS), ROWS)
            scaled[at, :] = (query_all[shard, rows, :].astype(F32) * factor).astype(BF16)
            return 0

        lax.fori_loop(0, tokens // ROWS, lap, 0)

    def scale_at(k):
        if k == 0:
            scale_query(me_c)
            return
        pl.when(me_c - k >= 0)(lambda: scale_query(me_c - k))
        pl.when(me_c + k < n_col)(lambda: scale_query(me_c + k))

    def x_next(at):
        for right in (True, False):
            @pl.when(x_sends(0, right))
            def _():
                x_send(0, sub_of(at, right), right).wait_send()
                x_send(0, sub_of(at + 1, right), right).start()

    def x_shards(k, at):
        for right in (True, False):
            piece = me_r - k if right else me_r + k
            sub = sub_of(at, right)
            yield right, piece * subs + sub, sub, (piece >= 0) if right else (piece < n_row)

    def x_arrive(k, at):
        for right, shard, sub, valid in x_shards(k, at):
            @pl.when(valid)
            def _():
                arrive(query_all.at[shard], x_recv.at[shard])
                if k < n_row - 1:
                    pl.when(x_sends(k, right))(lambda: x_send(k, sub, right).start())

    def x_product(k, at, p):
        for _, shard, _, valid in x_shards(k, at):
            pl.when(valid)(lambda: product(shard, 1, lambda: query_all[shard], p))

    def turn_gain(b, _):
        at = pl.ds(pl.multiple_of(b * LANES, LANES), LANES)
        column = as_column(gain[:, at], LANES)
        gain_column[at, :] = jnp.broadcast_to(column, (LANES, LANES))
        return 0

    def add_products(slot, shard, p):
        def step(rows):
            value = part[shard, p, rows, :].astype(F32) * gain[:, cols(p)]
            prods[slot, rows, :] += lane_sums(mid_all[shard, p, rows, :].astype(F32) * value)

        over_rows(step)

    def take_in(right, k, p):
        came = from_left if right else from_right
        recv = right_recv if right else left_recv
        pl.when(receives(right))(lambda: arrive(came.at[0, p], recv.at[k, p]))

    def add_in(right, k, p):
        if k == last:
            return
        came = from_left if right else from_right
        shard = me_c + last - k if right else me_c - last + k

        @pl.when(receives(right) & (k >= position(right)))
        def _():
            def step(rows):
                part[shard, p, rows, :] = (
                    part[shard, p, rows, :].astype(F32) + came[shard, p, rows, :].astype(F32)
                ).astype(BF16)

            over_rows(step)

    def start_index(right, index):
        if parts <= index < n_col * parts:
            start_out(right, index // parts, index % parts)

    def line_step(k, p):
        index = k * parts + p
        for right in (True, False):
            take_in(right, k, p)
            if ahead < parts:
                start_index(right, index + ahead)
            add_in(right, k, p)
            if ahead >= parts:
                start_index(right, index + ahead)
        if k == n_col - 2:
            pl.when(has_right)(lambda: add_products(1, me_c + 1, p))
            pl.when(has_left)(lambda: add_products(2, me_c - 1, p))

    def message_copy(right):
        slot = 0 if right else 1
        return push(
            message.at[slot], message_in.at[slot], msg_send.at[slot], msg_recv.at[slot],
            "col", me_c + 1 if right else me_c - 1,
        )

    def send_messages():
        for right in (True, False):
            slot = 0 if right else 1

            @pl.when(sends(right))
            def _():
                row = as_row(jnp.sum(prods[slot + 1], axis=1, keepdims=True))
                message[slot] = jnp.broadcast_to(row, (8, LANES))
                message_copy(right).start()

    def pr_copy(k):
        return push(
            prods_out, prods_in.at[me_r], pr_send.at[k], pr_recv.at[me_r],
            "row", lax.rem(me_r + k, n_row),
        )

    def send_products():
        row = as_row(jnp.sum(prods[0], axis=1, keepdims=True))
        prods_out[...] = jnp.broadcast_to(row, (8, LANES))
        for right in (True, False):
            slot = 0 if right else 1

            @pl.when(receives(right))
            def _():
                arrive(message_in.at[slot], msg_recv.at[slot])
                prods_out[...] += message_in[slot]

        for k in range(1, n_row):
            pr_copy(k).start()

    def take_products():
        summed = prods_out[...]
        for k in range(1, n_row):
            peer = lax.rem(me_r + k, n_row)
            arrive(prods_in.at[peer], pr_recv.at[peer])
            summed = summed + prods_in[peer]
        column = as_column(summed[:1], tokens)
        inverse = scales[me_c]
        scale[...] = inverse * inverse * inverse * (column / full)

    def weight(p):
        left = mid_all[:, p].reshape(n_col * tokens, fc)
        rows = pl.ds(p * fc, fc)
        factor = gain_column[rows, :]
        for at in range(0, depth, block):
            value = lax.dot_general(
                left, scaled[:, at : at + block], (((0,), (0,)), ((), ())),
                preferred_element_type=F32,
            )
            for b in range(0, block, LANES):
                grad_w[rows, at + b : at + b + LANES] = (value[:, b : b + LANES] * factor).astype(BF16)

    half = tokens // halves

    def term_copy(to, p, h):
        rows = pl.ds(h * half, half)
        return push(
            term.at[p, rows], later.at[me_s, p, rows], term_send.at[to, p, h],
            term_recv.at[me_s, p, h], "section", to,
        )

    def over_half(h, step):
        def lap(i, _):
            step(pl.ds(pl.multiple_of(h * half + i * ROWS, ROWS), ROWS))
            return 0

        lax.fori_loop(0, half // ROWS, lap, 0)

    def prepare(p):
        def step(rows):
            value = part[me_c, p, rows, :].astype(F32) * gain[:, cols(p)]
            total[p, rows, :] = (
                scales[me_c, rows, :][:, :1] * value
                - mid_all[me_c, p, rows, :].astype(F32) * scale[rows, :][:, :1]
            )

        over_rows(step)

    def finish(p):
        def step(rows):
            value = (
                from_left[me_c, p, rows, :].astype(F32)
                + from_right[me_c, p, rows, :].astype(F32)
            ) * gain[:, cols(p)]
            own = total[p, rows, :] + scales[me_c, rows, :][:, :1] * value
            term[p, rows, :] = own.astype(BF16)
            total[p, rows, :] = top[rows, cols(p)].astype(F32) + own

        for h in range(halves):
            over_half(h, step)
            for to in range(n_sec - 1):
                pl.when(me_s > to)(lambda: term_copy(to, p, h).start())

    def no_later():
        for source in range(1, n_sec):
            @pl.when(me_s >= source)
            def _():
                later[source] = jnp.zeros(later.shape[1:], BF16)

    def conclude(p):
        def step(rows):
            value = total[p, rows, :]
            for source in range(1, n_sec):
                value = value + later[source, p, rows, :].astype(F32)
            res[rows, cols(p)] = value.astype(BF16)

        for h in range(halves):
            for source in range(1, n_sec):
                @pl.when(me_s < source)
                def _():
                    rows = pl.ds(h * half, half)
                    arrive(later.at[source, p, rows], term_recv.at[source, p, h])

            over_half(h, step)

    def line_waits(right, slots):
        send = right_send if right else left_send
        for k in slots:
            for p in range(parts):
                arrive(part.at[0, p], send.at[k, p])

    def early_waits():
        for right in (True, False):
            for k in range(n_row - 1):
                @pl.when(x_sends(k, right))
                def _():
                    for at in range(subs - 1 if k == 0 else 0, subs):
                        x_send(k, sub_of(at, right), right).wait_send()

            pl.when(sends(right))(lambda: line_waits(right, range(last)))
            for k in range(last):
                pl.when(inverse_sends(right, k))(lambda: inverse_copy(right, k).wait_send())
        for k in range(1, n_row):
            sq_copy(k).wait_send()
            pr_copy(k).wait_send()

    def late_waits():
        for right in (True, False):
            @pl.when(sends(right))
            def _():
                line_waits(right, [last])
                message_copy(right).wait_send()
        for to in range(n_sec - 1):
            @pl.when(me_s > to)
            def _():
                for p in range(parts):
                    for h in range(halves):
                        term_copy(to, p, h).wait_send()

    query_in.wait()

    def own_lap(p, _):
        w_copy(p).wait()
        product(
            me_r * subs, subs, lambda: query_all[own_query].reshape(subs * tokens, depth), p
        )
        return 0

    lax.fori_loop(0, parts, own_lap, 0)
    for p in range(parts):
        mid_in(p).wait()
    square()
    gain_in.wait()
    blocks = width // LANES
    lax.fori_loop(0, blocks // 2, turn_gain, 0)
    if n_row > 1 and subs > 1:
        x_next(0)
    lax.fori_loop(blocks // 2, blocks, turn_gain, 0)

    @pl.when(jnp.logical_not(has_left))
    def _():
        from_left[me_c] = jnp.zeros(from_left.shape[1:], BF16)

    @pl.when(jnp.logical_not(has_right))
    def _():
        from_right[me_c] = jnp.zeros(from_right.shape[1:], BF16)

    steps = [(k, at) for k in range(1, n_row) for at in range(subs)]
    held = steps[-1:] if subs > 1 and n_col > 2 else []
    steps = steps[: len(steps) - len(held)]
    for k, at in steps[:-1]:
        x_arrive(k, at)
        for p in range(parts):
            x_product(k, at, p)
        if k == 1 and 0 < at < subs - 1:
            x_next(at)
    for p in range(parts):
        for k, at in steps[-1:]:
            if p == 0:
                x_arrive(k, at)
            x_product(k, at, p)
        if p == 0:
            prods[...] = jnp.zeros(prods.shape, F32)
        if n_col > 1:
            line_step(0, p)
        if p == min(1, parts - 1):
            own_inverse()
    if n_col > 1:
        pass_inverses(1)
    if n_col < 3:
        for p in range(parts):
            add_products(0, me_c, p)
    for k in range(1, last):
        for p in range(parts):
            for far, at in held if k == 1 else []:
                if p == 0:
                    x_arrive(far, at)
                x_product(far, at, p)
            line_step(k, p)
            if k == 1:
                add_products(0, me_c, p)
            if p == (1 if k == 1 and last > 2 else 0):
                pass_inverses(k + 1)
                if k == 1:
                    scale_at(0)
                scale_at(k)
                if k == last - 1:
                    scale_at(last)
            if k == last - 1:
                if p == parts - 1:
                    send_messages()
                weight(p)
    if 1 < n_col < 3:
        send_messages()
    if n_col < 3:
        for k in range(n_col):
            scale_at(k)
        for p in range(parts):
            weight(p)
    top_in.wait()
    no_later()
    done = 0
    for p in range(parts):
        if n_col > 1:
            line_step(last, p)
        if p == parts // 4:
            send_products()
        if p == parts // 2:
            take_products()
            for q in range(parts):
                prepare(q)
        if p >= parts // 2:
            while done <= p:
                finish(done)
                if done:
                    conclude(done - 1)
                done += 1
        if p == parts - 2:
            early_waits()
    if parts == 1:
        early_waits()
    conclude(parts - 1)
    late_waits()


def write_out(pieces, grad_w, res, grad_out, res_out, sem):
    tall = grad_w.shape[0] // pieces
    copies = [
        pltpu.make_async_copy(
            grad_w.at[pl.ds(i * tall, tall)], grad_out.at[pl.ds(i * tall, tall)], sem.at[i]
        )
        for i in range(pieces)
    ]
    copies.append(pltpu.make_async_copy(res, res_out, sem.at[pieces]))
    for copy in copies:
        copy.start()
    for copy in copies:
        copy.wait()


def body(mid, query_grad, top_grad, w_query, gain):
    n_sec, n_row, n_col = (lax.axis_size(a) for a in ("section", "row", "col"))
    tokens, width = mid.shape[1:]
    rows, depth = query_grad.shape[1:]
    subs = rows // tokens
    parts = PIECES
    fc = width // parts
    hbm = pl.BlockSpec(memory_space=pltpu.HBM)
    anywhere = pl.BlockSpec(memory_space=pl.ANY)
    in_vmem = pl.BlockSpec(memory_space=pltpu.VMEM)
    dma = pltpu.SemaphoreType.DMA
    vmem = pltpu.VMEM
    grad_w, res = pl.pallas_call(
        functools.partial(kernel, n_sec, n_row, n_col, parts, AHEAD, HALVES),
        out_shape=(vmem((width, depth), BF16), vmem((tokens, width), BF16)),
        in_specs=[hbm] * 5,
        out_specs=(in_vmem, in_vmem),
        scratch_shapes=[
            vmem((n_col, parts, tokens, fc), BF16),
            vmem((n_col, tokens, depth), BF16),
            vmem((n_col, parts, tokens, fc), BF16),
            vmem((n_col, parts, tokens, fc), BF16),
            vmem((n_col, parts, tokens, fc), BF16),
            vmem((n_col * tokens, depth), BF16),
            vmem((1, width), F32),
            vmem((width, LANES), F32),
            vmem((tokens, width), BF16),
            vmem((8, LANES), F32),
            vmem((n_row, 8, LANES), F32),
            vmem((n_col, 8, LANES), F32),
            vmem((n_col, tokens, LANES), F32),
            vmem((tokens, LANES), F32),
            vmem((3, tokens, LANES), F32),
            vmem((2, 8, LANES), F32),
            vmem((2, 8, LANES), F32),
            vmem((8, LANES), F32),
            vmem((n_row, 8, LANES), F32),
            vmem((parts, tokens, fc), BF16),
            vmem((n_sec, parts, tokens, fc), BF16),
            vmem((parts, tokens, fc), F32),
            dma((parts,)), dma, dma, dma, dma((parts,)),
            dma((n_col,)), dma((n_col,)), dma((n_col,)),
            dma((n_col, parts)), dma((n_col, parts)),
            dma((n_col, parts)), dma((n_col, parts)),
            dma((n_row,)), dma((n_row,)), dma((n_col,)), dma((n_col,)), dma((n_col,)),
            dma((2,)), dma((2,)), dma((n_row,)), dma((n_row,)),
            dma((n_sec, parts, HALVES)), dma((n_sec, parts, HALVES)),
        ],
        compiler_params=pltpu.CompilerParams(
            collective_id=0, has_side_effects=True, vmem_limit_bytes=40 * 1024 * 1024
        ),
    )(mid[0], query_grad[0].reshape(subs, tokens, depth), top_grad, gain, w_query[0])
    pieces = 8
    weight_grad, residual = pl.pallas_call(
        functools.partial(write_out, pieces),
        out_shape=(
            jax.ShapeDtypeStruct((width, depth), BF16),
            jax.ShapeDtypeStruct((tokens, width), BF16),
        ),
        in_specs=[anywhere] * 2,
        out_specs=(anywhere, anywhere),
        scratch_shapes=[dma((pieces + 1,))],
        compiler_params=pltpu.CompilerParams(vmem_limit_bytes=2 * 1024 * 1024),
    )(grad_w, res)
    return (weight_grad[None], residual[None])


def solution(mesh):
    return jax.shard_map(
        body,
        mesh=mesh,
        in_specs=(
            P("section", ("groups", "col"), "row"),
            P("section", ("groups", "row"), "col"),
            P(("groups", "col"), "row"),
            P("section", "row", "col"),
            P("section", "row"),
        ),
        out_specs=(P(("groups", "section"), "row", "col"), P("section", ("groups", "col"), "row")),
        check_vma=False,
    )
```

```python
import functools

import jax
import jax.numpy as jnp
from jax import lax
from jax.experimental import pallas as pl
from jax.experimental.pallas import tpu as pltpu
from jax.sharding import PartitionSpec as P

EPSILON = 1e-05
LANES = 128
ROWS = 16
PIECES = 4
AHEAD = 2
HALVES = 2
F32 = jnp.float32
BF16 = jnp.bfloat16
MESH = pl.DeviceIdType.MESH


def lane_sums(value):
    total = value[:, :LANES]
    for at in range(LANES, value.shape[1], LANES):
        total = total + value[:, at : at + LANES]
    return total


def diagonal(rows):
    shape = (rows, LANES)
    return lax.broadcasted_iota(jnp.int32, shape, 0) == lax.broadcasted_iota(jnp.int32, shape, 1)


def as_row(column):
    wide = jnp.broadcast_to(column, (column.shape[0], LANES))
    return jnp.sum(jnp.where(diagonal(column.shape[0]), wide, 0.0), axis=0, keepdims=True)


def as_column(row, rows):
    wide = jnp.broadcast_to(row, (rows, LANES))
    return jnp.sum(jnp.where(diagonal(rows), wide, 0.0), axis=1, keepdims=True)


def push(src, dst, send, recv, axis, peer):
    return pltpu.make_async_remote_copy(
        src_ref=src,
        dst_ref=dst,
        send_sem=send,
        recv_sem=recv,
        device_id={axis: peer},
        device_id_type=MESH,
    )


def arrive(ref, sem):
    pltpu.make_async_copy(ref, ref, sem).wait()


def kernel(
    n_sec, n_row, n_col, parts, ahead, halves,
    mid, query, top_hbm, gain_hbm, w_hbm,
    grad_w, res,
    mid_all, query_all, part, from_left, from_right, scaled, gain, gain_column, top,
    squares, squares_in, inverses, scales, scale,
    prods, message, message_in, prods_out, prods_in,
    term, later, total,
    mid_sem, query_sem, top_sem, gain_sem, w_sem,
    x_right, x_left, x_recv, right_send, right_recv, left_send, left_recv,
    sq_send, sq_recv, inv_right, inv_left, inv_recv, msg_send, msg_recv, pr_send, pr_recv, term_send, term_recv,
):
    me_s, me_r, me_c = (lax.axis_index(a) for a in ("section", "row", "col"))
    tokens, width = mid.shape
    subs, _, depth = query.shape
    fc = width // parts
    tile = min(1024, fc)
    block = min(512, depth)
    full = width * n_row
    last = n_col - 1
    has_left, has_right = me_c > 0, me_c < last

    def cols(p):
        return pl.ds(p * fc, fc)

    own_query = pl.ds(me_r * subs, subs)
    query_in = pltpu.make_async_copy(query, query_all.at[own_query], query_sem)
    gain_in = pltpu.make_async_copy(gain_hbm, gain, gain_sem)
    top_in = pltpu.make_async_copy(top_hbm, top, top_sem)

    def mid_in(p):
        return pltpu.make_async_copy(mid.at[:, cols(p)], mid_all.at[me_c, p], mid_sem.at[p])

    def w_copy(p):
        rows = pl.ds(pl.multiple_of(p * fc, fc), fc)
        return pltpu.make_async_copy(w_hbm.at[rows], grad_w.at[rows], w_sem.at[p])

    barrier = pltpu.get_barrier_semaphore()

    def greet(axis, peer):
        pl.semaphore_signal(barrier, inc=1, device_id={axis: peer}, device_id_type=MESH)

    for k in range(1, n_row):
        greet("row", lax.rem(me_r + k, n_row))
    pl.when(has_left)(lambda: greet("col", me_c - 1))
    pl.when(has_right)(lambda: greet("col", me_c + 1))
    for k in range(1, n_sec):
        greet("section", lax.rem(me_s + k, n_sec))
    query_in.start()
    gain_in.start()
    for p in range(parts):
        w_copy(p).start()
    for p in range(parts):
        mid_in(p).start()
    top_in.start()
    beside = (me_c + n_col - 1) // n_col + (2 * n_col - 2 - me_c) // n_col
    pl.semaphore_wait(barrier, n_row - 1 + n_sec - 1 + beside)

    def position(right):
        return me_c if right else last - me_c

    def sends(right):
        return has_right if right else has_left

    def receives(right):
        return has_left if right else has_right

    def line(src, dst, right, k, p):
        send, recv = (right_send, right_recv) if right else (left_send, left_recv)
        return push(
            src, dst, send.at[k, p], recv.at[k, p], "col", me_c + 1 if right else me_c - 1
        )

    def mid_copy(right, k, p):
        shard = me_c - k if right else me_c + k
        src = mid.at[:, cols(p)] if k == 0 else mid_all.at[shard, p]
        return line(src, mid_all.at[shard, p], right, k, p)

    def sum_copy(right, k, p):
        shard = me_c + n_col - k if right else me_c - n_col + k
        came = from_left if right else from_right
        return line(part.at[shard, p], came.at[shard, p], right, k, p)

    def start_out(right, k, p):
        if k == 0:
            pl.when(sends(right))(lambda: mid_copy(right, k, p).start())
            return
        early = k <= position(right)
        pl.when(sends(right) & early)(lambda: mid_copy(right, k, p).start())
        pl.when(sends(right) & jnp.logical_not(early))(lambda: sum_copy(right, k, p).start())

    for p in range(parts):
        for right in (True, False):
            start_out(right, 0, p)

    def x_send(k, sub, right):
        piece = me_r - k if right else me_r + k
        shard = piece * subs + sub
        src = query.at[sub] if k == 0 else query_all.at[shard]
        return push(
            src, query_all.at[shard], (x_right if right else x_left).at[shard], x_recv.at[shard],
            "row", me_r + 1 if right else me_r - 1,
        )

    def x_sends(k, right):
        if right:
            return (me_r - k >= 0) & (me_r < n_row - 1)
        return (me_r + k < n_row) & (me_r > 0)

    def sub_of(at, right):
        return at if right else subs - 1 - at

    for right in (True, False):
        pl.when(x_sends(0, right))(lambda: x_send(0, sub_of(0, right), right).start())

    def product(shard, count, load, p):
        for t in range(fc // tile):
            rows = pl.ds(pl.multiple_of(p * fc + t * tile, tile), tile)
            value = lax.dot_general(
                load(), grad_w[rows, :], (((1,), (1,)), ((), ())), preferred_element_type=F32
            ).astype(BF16)
            for at in range(count):
                part[shard + at, p, :, t * tile : (t + 1) * tile] = value[
                    at * tokens : (at + 1) * tokens
                ]

    def over_rows(step, count=tokens // ROWS):
        def lap(i, _):
            step(pl.ds(pl.multiple_of(i * ROWS, ROWS), ROWS))
            return 0

        lax.fori_loop(0, count, lap, 0)

    def sq_copy(k):
        return push(
            squares, squares_in.at[me_r], sq_send.at[k], sq_recv.at[me_r],
            "row", lax.rem(me_r + k, n_row),
        )

    def square():
        def step(rows):
            summed = jnp.zeros((ROWS, LANES), F32)
            for p in range(parts):
                value = mid_all[me_c, p, rows, :].astype(F32)
                summed = summed + lane_sums(value * value)
            prods[0, rows, :] = summed

        over_rows(step)
        row = as_row(jnp.sum(prods[0], axis=1, keepdims=True))
        squares[...] = jnp.broadcast_to(row, (8, LANES))
        for k in range(1, n_row):
            sq_copy(k).start()

    def inverse_copy(right, k):
        shard = me_c - k if right else me_c + k
        row = inverses.at[shard]
        return push(
            row, row, (inv_right if right else inv_left).at[shard], inv_recv.at[shard],
            "col", me_c + 1 if right else me_c - 1,
        )

    def inverse_sends(right, k):
        return (k <= position(right)) & sends(right)

    def own_inverse():
        summed = squares[...]
        for k in range(1, n_row):
            peer = lax.rem(me_r + k, n_row)
            arrive(squares_in.at[peer], sq_recv.at[peer])
            summed = summed + squares_in[peer]
        inverses[me_c] = lax.rsqrt(summed / full + EPSILON)
        for right in (True, False):
            pl.when(inverse_sends(right, 0))(lambda: inverse_copy(right, 0).start())

    def pass_inverses(k):
        for right in (True, False):
            shard = me_c - k if right else me_c + k

            @pl.when((shard >= 0) if right else (shard < n_col))
            def _():
                arrive(inverses.at[shard], inv_recv.at[shard])
                if k < last:
                    pl.when(inverse_sends(right, k))(lambda: inverse_copy(right, k).start())

    def scale_query(shard):
        column = as_column(inverses[shard, :1, :], tokens)
        scales[shard] = jnp.broadcast_to(column, (tokens, LANES))

        def lap(i, _):
            rows = pl.ds(pl.multiple_of(i * ROWS, ROWS), ROWS)
            factor = scales[shard, rows, :][:, :1] * (n_col * tokens) ** -0.5
            at = pl.ds(pl.multiple_of(shard * tokens + i * ROWS, ROWS), ROWS)
            scaled[at, :] = (query_all[shard, rows, :].astype(F32) * factor).astype(BF16)
            return 0

        lax.fori_loop(0, tokens // ROWS, lap, 0)

    def scale_at(k):
        if k == 0:
            scale_query(me_c)
            return
        pl.when(me_c - k >= 0)(lambda: scale_query(me_c - k))
        pl.when(me_c + k < n_col)(lambda: scale_query(me_c + k))

    def x_next(at):
        for right in (True, False):
            @pl.when(x_sends(0, right))
            def _():
                x_send(0, sub_of(at, right), right).wait_send()
                x_send(0, sub_of(at + 1, right), right).start()

    def x_shards(k, at):
        for right in (True, False):
            piece = me_r - k if right else me_r + k
            sub = sub_of(at, right)
            yield right, piece * subs + sub, sub, (piece >= 0) if right else (piece < n_row)

    def x_arrive(k, at):
        for right, shard, sub, valid in x_shards(k, at):
            @pl.when(valid)
            def _():
                arrive(query_all.at[shard], x_recv.at[shard])
                if k < n_row - 1:
                    pl.when(x_sends(k, right))(lambda: x_send(k, sub, right).start())

    def x_product(k, at, p):
        for _, shard, _, valid in x_shards(k, at):
            pl.when(valid)(lambda: product(shard, 1, lambda: query_all[shard], p))

    def turn_gain(b, _):
        at = pl.ds(pl.multiple_of(b * LANES, LANES), LANES)
        column = as_column(gain[:, at], LANES)
        gain_column[at, :] = jnp.broadcast_to(column, (LANES, LANES))
        return 0

    def add_products(slot, shard, p):
        def step(rows):
            value = part[shard, p, rows, :].astype(F32) * gain[:, cols(p)]
            prods[slot, rows, :] += lane_sums(mid_all[shard, p, rows, :].astype(F32) * value)

        over_rows(step)

    def take_in(right, k, p):
        came = from_left if right else from_right
        recv = right_recv if right else left_recv
        pl.when(receives(right))(lambda: arrive(came.at[0, p], recv.at[k, p]))

    def add_in(right, k, p):
        if k == last:
            return
        came = from_left if right else from_right
        shard = me_c + last - k if right else me_c - last + k

        @pl.when(receives(right) & (k >= position(right)))
        def _():
            def step(rows):
                part[shard, p, rows, :] = (
                    part[shard, p, rows, :].astype(F32) + came[shard, p, rows, :].astype(F32)
                ).astype(BF16)

            over_rows(step)

    def start_index(right, index):
        if parts <= index < n_col * parts:
            start_out(right, index // parts, index % parts)

    def line_step(k, p):
        index = k * parts + p
        for right in (True, False):
            take_in(right, k, p)
            if ahead < parts - 1:
                for more, mine in ((0, me_s == 0), (1, me_s > 0)):
                    pl.when(mine)(lambda: start_index(right, index + ahead + more))
            elif ahead < parts:
                start_index(right, index + ahead)
            add_in(right, k, p)
            if ahead >= parts:
                start_index(right, index + ahead)
        if k == n_col - 2:
            pl.when(has_right)(lambda: add_products(1, me_c + 1, p))
            pl.when(has_left)(lambda: add_products(2, me_c - 1, p))

    def message_copy(right):
        slot = 0 if right else 1
        return push(
            message.at[slot], message_in.at[slot], msg_send.at[slot], msg_recv.at[slot],
            "col", me_c + 1 if right else me_c - 1,
        )

    def send_messages():
        for right in (True, False):
            slot = 0 if right else 1

            @pl.when(sends(right))
            def _():
                row = as_row(jnp.sum(prods[slot + 1], axis=1, keepdims=True))
                message[slot] = jnp.broadcast_to(row, (8, LANES))
                message_copy(right).start()

    def pr_copy(k):
        return push(
            prods_out, prods_in.at[me_r], pr_send.at[k], pr_recv.at[me_r],
            "row", lax.rem(me_r + k, n_row),
        )

    def send_products():
        row = as_row(jnp.sum(prods[0], axis=1, keepdims=True))
        prods_out[...] = jnp.broadcast_to(row, (8, LANES))
        for right in (True, False):
            slot = 0 if right else 1

            @pl.when(receives(right))
            def _():
                arrive(message_in.at[slot], msg_recv.at[slot])
                prods_out[...] += message_in[slot]

        for k in range(1, n_row):
            pr_copy(k).start()

    def take_products():
        summed = prods_out[...]
        for k in range(1, n_row):
            peer = lax.rem(me_r + k, n_row)
            arrive(prods_in.at[peer], pr_recv.at[peer])
            summed = summed + prods_in[peer]
        column = as_column(summed[:1], tokens)
        inverse = scales[me_c]
        scale[...] = inverse * inverse * inverse * (column / full)

    def weight(p):
        left = mid_all[:, p].reshape(n_col * tokens, fc)
        rows = pl.ds(p * fc, fc)
        factor = gain_column[rows, :]
        for at in range(0, depth, block):
            value = lax.dot_general(
                left, scaled[:, at : at + block], (((0,), (0,)), ((), ())),
                preferred_element_type=F32,
            )
            for b in range(0, block, LANES):
                grad_w[rows, at + b : at + b + LANES] = (value[:, b : b + LANES] * factor).astype(BF16)

    half = tokens // halves

    def term_copy(to, p, h):
        rows = pl.ds(h * half, half)
        return push(
            term.at[p, rows], later.at[me_s, p, rows], term_send.at[to, p, h],
            term_recv.at[me_s, p, h], "section", to,
        )

    def over_half(h, step):
        def lap(i, _):
            step(pl.ds(pl.multiple_of(h * half + i * ROWS, ROWS), ROWS))
            return 0

        lax.fori_loop(0, half // ROWS, lap, 0)

    def finish(p):
        def step(rows):
            value = (
                part[me_c, p, rows, :].astype(F32)
                + from_left[me_c, p, rows, :].astype(F32)
                + from_right[me_c, p, rows, :].astype(F32)
            ) * gain[:, cols(p)]
            own = (
                scales[me_c, rows, :][:, :1] * value
                - mid_all[me_c, p, rows, :].astype(F32) * scale[rows, :][:, :1]
            )
            term[p, rows, :] = own.astype(BF16)
            total[p, rows, :] = top[rows, cols(p)].astype(F32) + own

        for h in range(halves):
            over_half(h, step)
            for to in range(n_sec - 1):
                pl.when(me_s > to)(lambda: term_copy(to, p, h).start())

    def no_later():
        for source in range(1, n_sec):
            @pl.when(me_s >= source)
            def _():
                later[source] = jnp.zeros(later.shape[1:], BF16)

    def conclude(p):
        def step(rows):
            value = total[p, rows, :]
            for source in range(1, n_sec):
                value = value + later[source, p, rows, :].astype(F32)
            res[rows, cols(p)] = value.astype(BF16)

        for h in range(halves):
            for source in range(1, n_sec):
                @pl.when(me_s < source)
                def _():
                    rows = pl.ds(h * half, half)
                    arrive(later.at[source, p, rows], term_recv.at[source, p, h])

            over_half(h, step)

    def line_waits(right, slots):
        send = right_send if right else left_send
        for k in slots:
            for p in range(parts):
                arrive(part.at[0, p], send.at[k, p])

    def early_waits():
        for right in (True, False):
            for k in range(n_row - 1):
                @pl.when(x_sends(k, right))
                def _():
                    for at in range(subs - 1 if k == 0 else 0, subs):
                        x_send(k, sub_of(at, right), right).wait_send()

            pl.when(sends(right))(lambda: line_waits(right, range(last)))
            for k in range(last):
                pl.when(inverse_sends(right, k))(lambda: inverse_copy(right, k).wait_send())
        for k in range(1, n_row):
            sq_copy(k).wait_send()
            pr_copy(k).wait_send()

    def late_waits():
        for right in (True, False):
            @pl.when(sends(right))
            def _():
                line_waits(right, [last])
                message_copy(right).wait_send()
        for to in range(n_sec - 1):
            @pl.when(me_s > to)
            def _():
                for p in range(parts):
                    for h in range(halves):
                        term_copy(to, p, h).wait_send()

    query_in.wait()

    def own_lap(p, _):
        w_copy(p).wait()
        product(
            me_r * subs, subs, lambda: query_all[own_query].reshape(subs * tokens, depth), p
        )
        return 0

    lax.fori_loop(0, parts, own_lap, 0)
    for p in range(parts):
        mid_in(p).wait()
    square()
    gain_in.wait()
    blocks = width // LANES
    lax.fori_loop(0, blocks // 2, turn_gain, 0)
    if n_row > 1 and subs > 1:
        x_next(0)
    lax.fori_loop(blocks // 2, blocks, turn_gain, 0)

    @pl.when(jnp.logical_not(has_left))
    def _():
        from_left[me_c] = jnp.zeros(from_left.shape[1:], BF16)

    @pl.when(jnp.logical_not(has_right))
    def _():
        from_right[me_c] = jnp.zeros(from_right.shape[1:], BF16)

    steps = [(k, at) for k in range(1, n_row) for at in range(subs)]
    held = steps[-1:] if subs > 1 and n_col > 2 else []
    steps = steps[: len(steps) - len(held)]
    for k, at in steps[:-1]:
        x_arrive(k, at)
        for p in range(parts):
            x_product(k, at, p)
        if k == 1 and 0 < at < subs - 1:
            x_next(at)
    for p in range(parts):
        for k, at in steps[-1:]:
            if p == 0:
                x_arrive(k, at)
            x_product(k, at, p)
        if p == 0:
            prods[...] = jnp.zeros(prods.shape, F32)
        if n_col > 1:
            line_step(0, p)
        if p == min(1, parts - 1):
            own_inverse()
    if n_col > 1:
        pass_inverses(1)
    if n_col < 3:
        for p in range(parts):
            add_products(0, me_c, p)
    for k in range(1, last):
        for p in range(parts):
            for far, at in held if k == 1 else []:
                if p == 0:
                    x_arrive(far, at)
                x_product(far, at, p)
            line_step(k, p)
            if k == 1:
                add_products(0, me_c, p)
            if p == (1 if k == 1 and last > 2 else 0):
                pass_inverses(k + 1)
                if k == 1:
                    scale_at(0)
                scale_at(k)
                if k == last - 1:
                    scale_at(last)
            if k == last - 1:
                if p == parts - 1:
                    send_messages()
                weight(p)
    if 1 < n_col < 3:
        send_messages()
    if n_col < 3:
        for k in range(n_col):
            scale_at(k)
        for p in range(parts):
            weight(p)
    top_in.wait()
    no_later()
    done = 0
    for p in range(parts):
        if n_col > 1:
            line_step(last, p)
        if p == parts // 4:
            send_products()
        if p == parts // 2:
            take_products()
        if p >= parts // 2:
            while done <= p:
                finish(done)
                if done:
                    conclude(done - 1)
                done += 1
        if p == parts - 2:
            early_waits()
    if parts == 1:
        early_waits()
    conclude(parts - 1)
    late_waits()


def write_out(pieces, grad_w, res, grad_out, res_out, sem):
    tall = grad_w.shape[0] // pieces
    copies = [
        pltpu.make_async_copy(
            grad_w.at[pl.ds(i * tall, tall)], grad_out.at[pl.ds(i * tall, tall)], sem.at[i]
        )
        for i in range(pieces)
    ]
    copies.append(pltpu.make_async_copy(res, res_out, sem.at[pieces]))
    for copy in copies:
        copy.start()
    for copy in copies:
        copy.wait()


def body(mid, query_grad, top_grad, w_query, gain):
    n_sec, n_row, n_col = (lax.axis_size(a) for a in ("section", "row", "col"))
    tokens, width = mid.shape[1:]
    rows, depth = query_grad.shape[1:]
    subs = rows // tokens
    parts = PIECES
    fc = width // parts
    hbm = pl.BlockSpec(memory_space=pltpu.HBM)
    anywhere = pl.BlockSpec(memory_space=pl.ANY)
    in_vmem = pl.BlockSpec(memory_space=pltpu.VMEM)
    dma = pltpu.SemaphoreType.DMA
    vmem = pltpu.VMEM
    grad_w, res = pl.pallas_call(
        functools.partial(kernel, n_sec, n_row, n_col, parts, AHEAD, HALVES),
        out_shape=(vmem((width, depth), BF16), vmem((tokens, width), BF16)),
        in_specs=[hbm] * 5,
        out_specs=(in_vmem, in_vmem),
        scratch_shapes=[
            vmem((n_col, parts, tokens, fc), BF16),
            vmem((n_col, tokens, depth), BF16),
            vmem((n_col, parts, tokens, fc), BF16),
            vmem((n_col, parts, tokens, fc), BF16),
            vmem((n_col, parts, tokens, fc), BF16),
            vmem((n_col * tokens, depth), BF16),
            vmem((1, width), F32),
            vmem((width, LANES), F32),
            vmem((tokens, width), BF16),
            vmem((8, LANES), F32),
            vmem((n_row, 8, LANES), F32),
            vmem((n_col, 8, LANES), F32),
            vmem((n_col, tokens, LANES), F32),
            vmem((tokens, LANES), F32),
            vmem((3, tokens, LANES), F32),
            vmem((2, 8, LANES), F32),
            vmem((2, 8, LANES), F32),
            vmem((8, LANES), F32),
            vmem((n_row, 8, LANES), F32),
            vmem((parts, tokens, fc), BF16),
            vmem((n_sec, parts, tokens, fc), BF16),
            vmem((parts, tokens, fc), F32),
            dma((parts,)), dma, dma, dma, dma((parts,)),
            dma((n_col,)), dma((n_col,)), dma((n_col,)),
            dma((n_col, parts)), dma((n_col, parts)),
            dma((n_col, parts)), dma((n_col, parts)),
            dma((n_row,)), dma((n_row,)), dma((n_col,)), dma((n_col,)), dma((n_col,)),
            dma((2,)), dma((2,)), dma((n_row,)), dma((n_row,)),
            dma((n_sec, parts, HALVES)), dma((n_sec, parts, HALVES)),
        ],
        compiler_params=pltpu.CompilerParams(
            collective_id=0, has_side_effects=True, vmem_limit_bytes=40 * 1024 * 1024
        ),
    )(mid[0], query_grad[0].reshape(subs, tokens, depth), top_grad, gain, w_query[0])
    pieces = 8
    weight_grad, residual = pl.pallas_call(
        functools.partial(write_out, pieces),
        out_shape=(
            jax.ShapeDtypeStruct((width, depth), BF16),
            jax.ShapeDtypeStruct((tokens, width), BF16),
        ),
        in_specs=[anywhere] * 2,
        out_specs=(anywhere, anywhere),
        scratch_shapes=[dma((pieces + 1,))],
        compiler_params=pltpu.CompilerParams(vmem_limit_bytes=2 * 1024 * 1024),
    )(grad_w, res)
    return (weight_grad[None], residual[None])


def solution(mesh):
    return jax.shard_map(
        body,
        mesh=mesh,
        in_specs=(
            P("section", ("groups", "col"), "row"),
            P("section", ("groups", "row"), "col"),
            P(("groups", "col"), "row"),
            P("section", "row", "col"),
            P("section", "row"),
        ),
        out_specs=(P(("groups", "section"), "row", "col"), P("section", ("groups", "col"), "row")),
        check_vma=False,
    )
```
